32 devices in a mesh: groups: 2 (over y), segment: 4 (over z), dp: 4 (over x, core).
Axes of the slice: x: 2, y: 2, z: 4, core: 2. Of those that a mesh axis runs over, the one named last changes fastest.
Arguments:
- hidden: bfloat16 [4, 1152, 512], P('segment', ('groups', 'dp')), parts along dimension 1, may hold values from -6 to 6
- stash: bfloat16 [4, 2, 1152, 512], P('segment', None, ('groups', 'dp')), parts along dimension 2, may hold values from -6 to 6
- skip_store: bfloat16 [4, 2, 1152, 512], P('segment', None, ('groups', 'dp')), parts along dimension 2, may hold values from -6 to 6
- cotan: bfloat16 [4, 1152, 512], P('segment', ('groups', 'dp')), parts along dimension 1, may hold values from -6 to 6
- entry: bfloat16 [1, 1152, 512], P(None, ('groups', 'dp')), parts along dimension 1, may hold values from -6 to 6
- loss_grad: bfloat16 [1, 1152, 512], P(None, ('groups', 'dp')), parts along dimension 1, may hold values from -6 to 6
- wqkv: bfloat16 [4, 512, 1536], P('segment', 'dp')
- wout: bfloat16 [4, 512, 512], P('segment', 'dp'), may hold values from -0.25 to 0.25
- region: int32 [4, 1152], P('segment', ('groups', 'dp')), parts along dimension 1, may hold values from 0 to 3
Outputs:
- acts_out: bfloat16 [4, 1152, 512], P('segment', ('groups', 'dp')), parts along dimension 1
- grads_out: bfloat16 [4, 1152, 512], P('segment', ('groups', 'dp')), parts along dimension 1
- grad_qkv: float32 [8, 512, 1536], P(('groups', 'segment'), 'dp'), parts along dimension 0
- grad_out_proj: float32 [8, 512, 512], P(('groups', 'segment'), 'dp'), parts along dimension 0
The draws below stay inside these ranges and needn't reach their ends.
There are 2 independent parts, one for each index of `groups`. The reference program is written for one: setup_inputs(seed, part) draws one part's arguments, and reference() takes and returns one part's arrays. A program takes and returns all parts, laid end to end along the dimension named above; an argument that names none is the same for every part. Nothing has to cross between parts.
All inputs are finite; a program needn't handle non-finite values.
Results may differ from the reference program's by a relative error of at most 0.025.
The reference program's roundings to bfloat16 on the way count: a program that leaves them out, or rounds other values in their place, can miss the bound.
Values may be sent and summed in bfloat16 or wider, within the bound.
A program may use at most 64 MiB of HBM per device.

```python
import jax
import jax.numpy as jnp
from jax import lax

HEADS = 8
HEAD_DIM = 64
D = 512
WINDOW = 144
TICKS = 2
SEGMENTS = 4
TOKENS = 576
N_DP = 4


def draw_wqkv(key, part):
    base = jax.random.normal(key, (SEGMENTS, D, 3 * D), jnp.float32) * D ** (-0.5)
    return base.astype(jnp.bfloat16)


def place_ends(values, stream_key, smallest, high):
    index_at = [jax.random.randint(jax.random.fold_in(stream_key, axis), (), 0, length) for axis, length in enumerate(values.shape)]
    main_axis = values.shape.index(max(values.shape))
    next_to = index_at[:main_axis] + [(index_at[main_axis] + 1) % values.shape[main_axis]] + index_at[main_axis + 1:]
    return values.at[tuple(index_at)].set(smallest).at[tuple(next_to)].set(high)


def level_of(own_key, dims, pieces, least, high):
    def one(axis_at, shards_of):
        draws = jax.random.uniform(jax.random.fold_in(jax.random.fold_in(own_key, 6), axis_at), (shards_of,), jnp.float32, least / len(pieces), high / len(pieces))
        return jnp.repeat(jnp.exp(draws), dims[axis_at] // shards_of).reshape((-1,) + (1,) * (len(dims) - axis_at - 1))

    factor_of = one(*pieces[0])
    for cut in pieces[1:]:
        factor_of = factor_of * one(*cut)
    return factor_of


def bell_draw(key, shape, deviation, bound, shards=(), kind=jnp.bfloat16):
    array = jax.random.normal(key, shape, jnp.float32) * deviation
    if len(shards) > 0:
        array = level_of(key, shape, shards, -0.22, 0.18) * array
    return jnp.clip(array, min=-bound, max=bound).astype(kind)


def setup_inputs(seed: int = 0, part: int = 0) -> dict:
    key_list = jax.random.split(jax.random.key(seed), 10)
    own_keys = jax.random.split(jax.random.fold_in(key_list[9], part), 10)
    return {
        "hidden": bell_draw(own_keys[0], (SEGMENTS, TOKENS, D), 1.0, 6.0, ((0, 4), (1, 4))),
        "stash": bell_draw(own_keys[1], (SEGMENTS, TICKS, TOKENS, D), 1.0, 6.0, ((0, 4), (2, 4))),
        "skip_store": bell_draw(own_keys[2], (SEGMENTS, TICKS, TOKENS, D), 1.0, 6.0, ((0, 4), (2, 4))),
        "cotan": bell_draw(own_keys[3], (SEGMENTS, TOKENS, D), 1.0, 6.0, ((0, 4), (1, 4))),
        "entry": bell_draw(own_keys[4], (TICKS - 1, TOKENS, D), 1.0, 6.0, ((1, 4),)),
        "loss_grad": bell_draw(own_keys[5], (TICKS - 1, TOKENS, D), 1.0, 6.0, ((1, 4),)),
        "wqkv": draw_wqkv(jax.random.fold_in(key_list[9], 71), part),
        "wout": bell_draw(key_list[7], (SEGMENTS, D, D), D ** -0.5, 0.25, ((0, 4), (1, 4))),
        "region": place_ends(jax.random.randint(own_keys[8], (SEGMENTS, TOKENS), 0, 4), jax.random.fold_in(own_keys[8], 1), 0, 3).astype(jnp.int32),
    }


def attend_block(u, wqkv, wout, region):
    row_count, features = u.shape
    windows = row_count // WINDOW
    upcast = u.astype(jnp.float32)
    centred = upcast - lax.optimization_barrier(jnp.mean(upcast, axis=-1, keepdims=True))
    normed = (centred * lax.rsqrt(lax.optimization_barrier(jnp.mean(centred * centred, axis=-1, keepdims=True)) + 1e-05)).astype(jnp.bfloat16)
    projected = jnp.dot(normed, wqkv, preferred_element_type=jnp.float32).astype(jnp.bfloat16)
    queries = projected[:, :features].reshape(windows, WINDOW, HEADS, HEAD_DIM)
    keys_all = projected[:, features:2 * features].reshape(windows, WINDOW, HEADS, HEAD_DIM)
    values = projected[:, 2 * features:].reshape(windows, WINDOW, HEADS, HEAD_DIM)
    scores = jnp.einsum('wqhd,wkhd->whqk', queries.astype(jnp.float32), keys_all.astype(jnp.float32)) * HEAD_DIM ** (-0.5)
    labels = region.reshape(windows, WINDOW)
    allowed = labels[:, None, :, None] == labels[:, None, None, :]
    scores = jnp.where(allowed, scores, jnp.float32(-1000000000.0))
    weights = jax.nn.softmax(scores, axis=-1).astype(jnp.bfloat16)
    context = jnp.einsum('whqk,wkhd->wqhd', weights.astype(jnp.float32), values.astype(jnp.float32))
    context = context.astype(jnp.bfloat16).reshape(row_count, features)
    return (upcast + jnp.dot(context, wout, preferred_element_type=jnp.float32)).astype(jnp.bfloat16)

def reference(hidden, stash, skip_store, cotan, entry, loss_grad, wqkv, wout, region):
    segments = hidden.shape[0]
    features = hidden.shape[-1]
    decoder = (jnp.arange(segments) >= segments // 2)[:, None, None]
    mirrored = skip_store[::-1]
    inputs = hidden
    grads_in = cotan
    grad_qkv = jnp.zeros(wqkv.shape, jnp.float32)
    grad_proj = jnp.zeros(wout.shape, jnp.float32)
    outputs = hidden
    grad_acts = cotan
    for tick_no in range(TICKS):
        if tick_no > 0:
            inputs = jnp.concatenate([entry[tick_no - 1][None], outputs[:-1]], axis=0)
            grads_in = jnp.concatenate([grad_acts[1:], loss_grad[tick_no - 1][None]], axis=0)
        summed = (inputs.astype(jnp.float32) + mirrored[:, tick_no].astype(jnp.float32)).astype(jnp.bfloat16)
        joined = jnp.where(decoder, summed, inputs)

        def per_section(packed):
            acts, stored, cotangent, w_qkv, w_out, labels = packed
            acts = acts.reshape(N_DP, -1, features)
            stored = stored.reshape(N_DP, -1, features)
            cotangent = cotangent.reshape(N_DP, -1, features)
            labels = labels.reshape(N_DP, -1)
            result = jax.vmap(lambda a, r: attend_block(a, w_qkv, w_out, r))(acts, labels)

            def backward(a, c, r):
                _, pullback = jax.vjp(lambda x, p, q: attend_block(x, p, q, r), a, w_qkv, w_out)
                return pullback(c)
            d_acts, d_qkv, d_out = jax.vmap(backward)(stored, cotangent, labels)
            return (result.reshape(-1, features), d_acts.reshape(-1, features), lax.optimization_barrier(jnp.sum(d_qkv.astype(jnp.float32), axis=0)), lax.optimization_barrier(jnp.sum(d_out.astype(jnp.float32), axis=0)))
        outputs, grad_acts, step_qkv, step_out = lax.map(per_section, (joined, stash[:, tick_no], grads_in, wqkv, wout, region))
        grad_qkv = grad_qkv + step_qkv
        grad_proj = grad_proj + step_out
    return (outputs, grad_acts, grad_qkv, grad_proj)
```

```python
import functools

import jax
import jax.numpy as jnp
from jax import lax
from jax.experimental import pallas as pl
from jax.experimental.pallas import tpu as pltpu
from jax.sharding import PartitionSpec as P

HEADS = 8
HEAD_DIM = 64
WINDOW = 144
PAIR = 2 * HEAD_DIM
PAIRS = HEADS // 2
BF = jnp.bfloat16
F32 = jnp.float32
MESH = pl.DeviceIdType.MESH


def mm(a, b, ca=1, cb=0):
    return lax.dot_general(a, b, (((ca,), (cb,)), ((), ())), preferred_element_type=F32)


def stats(u):
    up = u.astype(F32)
    centred = up - jnp.mean(up, axis=-1, keepdims=True)
    scale = lax.rsqrt(jnp.mean(centred * centred, axis=-1, keepdims=True) + 1e-05)
    return centred * scale, scale


def flush(*refs):
    srcs, dsts, sems = refs[0:4], refs[4:8], refs[8]
    stores = [pltpu.make_async_copy(srcs[i], dsts[i], sems.at[i]) for i in range(4)]
    for store in stores:
        store.start()
    for store in stores:
        store.wait()


def kernel(n, segs, hid_in, stash_in, skip, cot_in, ent_in, lgrad_in, wq, wo, reg_in,
           acts, grads, gq, go,
           hid, stash, cot, ent, lgrad, reg, lsem,
           wqf, wof, skin, yin, ysend, din, dsend, joined, gall, nrm, proj, nt, ct, dproj, ctx,
           prob, same2,
           q1s, q1r, qkeep, q2s, q2r, o1s, o1r, okeep, o2s, o2r,
           xs, xr, ys, yr, cs, cr, es, er, ms, mr, ksend, krecv, rsend, rrecv, p1s, p1r, p2s, p2r, ready):
    rows, width = hid_in.shape[1], hid_in.shape[2]
    half = n // 2
    depth = wq.shape[1]
    me = lax.axis_index("dp")
    seg = lax.axis_index("segment")
    grp = lax.axis_index("groups")
    chip, core = me // 2, me % 2
    other = 1 - core
    mate = chip * 2 + other
    mirror = segs - 1 - seg
    decoder = seg >= segs // 2

    def peer(off):
        return lax.rem(chip + off, half)

    loads = [pltpu.make_async_copy(src, dst, lsem.at[i]) for i, (src, dst) in enumerate((
        (stash_in, stash), (hid_in, hid), (cot_in, cot), (reg_in, reg),
        (wq.at[0], wqf.at[me]), (wo.at[0], wof.at[me]), (ent_in, ent), (lgrad_in, lgrad)))]
    for load in loads:
        load.start()

    barrier = pltpu.get_barrier_semaphore()

    def greet(**where):
        pl.semaphore_signal(barrier, inc=1, device_id=where, device_id_type=MESH)

    greet(dp=mate)
    greet(groups=1 - grp)
    for off in range(1, half):
        greet(dp=peer(off) * 2 + core)
    @pl.when(seg > 0)
    def _():
        greet(segment=seg - 1)

    @pl.when(seg < segs - 1)
    def _():
        greet(segment=seg + 1)

    count = half + 1 + jnp.where(seg > 0, 1, 0)
    pl.semaphore_wait(barrier, count + jnp.where(seg < segs - 1, 1, 0))

    def announce():
        pl.semaphore_signal(ready, inc=1, device_id={"segment": seg - 1}, device_id_type=MESH)

    if segs > 2:
        @pl.when(seg == segs - 2)
        def _():
            announce()

    def begin_skip():
        @pl.when(seg < segs - 2)
        def _():
            pl.semaphore_wait(ready, 1)

        @pl.when(jnp.logical_and(seg < segs - 2, seg > 0))
        def _():
            announce()

        @pl.when(jnp.logical_not(decoder))
        def _():
            skip_copy(0).start()
            skip_copy(1).start()

    def remote(src, dst, ssem, rsem, **where):
        return pltpu.make_async_remote_copy(
            src_ref=src, dst_ref=dst, send_sem=ssem, recv_sem=rsem,
            device_id=where, device_id_type=MESH)

    fulls, shards = (wqf, wof), (wq, wo)
    span = depth // 2
    pieces = [(w, at, size) for w, size in ((0, 16), (1, 32)) for at in range(0, span, size)]
    first = sum(1 for w, _, _ in pieces if w == 0)
    sent = []

    def rows_of(ref, lead, k, group):
        _, at, size = pieces[k]
        return ref.at[lead, pl.ds(pl.multiple_of(group * span + at, size), size)]

    def send(copy):
        copy.start()
        sent.append(copy)

    for k, (w, _, _) in enumerate(pieces):
        for off in range(1, half):
            send(remote(rows_of(shards[w], 0, k, grp), rows_of(fulls[w], me, k, grp),
                        xs.at[off, k], xr.at[chip, k], dp=peer(off) * 2 + core))
    for w in range(2):
        send(remote(shards[w].at[0], fulls[w].at[me], ms.at[w], mr.at[w], dp=mate))

    def pass_on(k, off, group, ssem, rsem, **where):
        w, src = pieces[k][0], peer(off) * 2 + core
        block = rows_of(fulls[w], src, k, group)
        return remote(block, block, ssem.at[peer(off), k], rsem.at[peer(off), k], **where)

    def from_x(k):
        for off in range(1, half):
            pass_on(k, off, grp, xs, xr, dp=mate).wait_recv()
            send(pass_on(k, off, grp, ys, yr, groups=1 - grp))
            send(pass_on(k, off, grp, cs, cr, dp=mate))

    def from_y(k):
        for off in range(1, half):
            pass_on(k, off, 1 - grp, ys, yr, groups=1 - grp).wait_recv()
            send(pass_on(k, off, 1 - grp, es, er, dp=mate))

    def from_core(k):
        w = pieces[k][0]
        for off in range(1, half):
            for group, rsem in ((grp, cr), (1 - grp, er)):
                block = rows_of(fulls[w], peer(off) * 2 + other, k, group)
                remote(block, block, cs.at[peer(off), k], rsem.at[peer(off), k],
                       dp=mate).wait_recv()

    def from_mate(w):
        block = fulls[w].at[mate]
        remote(block, block, ms.at[w], mr.at[w], dp=mate).wait_recv()

    def skip_copy(t):
        return remote(skip.at[0, t], skin.at[t], ksend.at[t], krecv.at[t], segment=mirror)

    for load in loads:
        load.wait()

    labels = jnp.broadcast_to(reg[...], (16, rows))
    onehot = (lax.broadcasted_iota(jnp.int32, (16, rows), 0) == labels).astype(F32).astype(BF)
    same = mm(onehot, onehot, 0, 0)
    same2[0:rows] = same
    same2[rows:2 * rows] = same
    lane = lax.broadcasted_iota(jnp.int32, (rows, PAIR), 1) < HEAD_DIM
    lo = lane.astype(F32).astype(BF)
    hi = (1.0 - lane.astype(F32)).astype(BF)

    def stack(x):
        return jnp.concatenate([x * lo, x * hi], axis=0)

    def fold(x):
        return jnp.where(lane, x[:rows], x[rows:])

    def part(row0, p, which):
        return proj[row0:row0 + rows, which * width + p * PAIR:which * width + (p + 1) * PAIR]

    def softmax(row0, p):
        scores = mm(stack(part(row0, p, 0)), part(row0, p, 1), 1, 1) * HEAD_DIM ** (-0.5)
        scores = jnp.where(same2[...] > 0.5, scores, F32(-1000000000.0))
        e = jnp.exp(scores - jnp.max(scores, axis=-1, keepdims=True))
        return e * (1.0 / jnp.sum(e, axis=-1, keepdims=True))

    def by_owner(x, dest):
        for c in range(2):
            cols = [x[:, (2 * k + c) * depth:(2 * k + c + 1) * depth] for k in range(half)]
            dest[c] = jnp.concatenate(cols, axis=1).T

    for t in range(2):
        nrm[(1 + t) * rows:(2 + t) * rows] = stats(stash[0, t])[0].astype(BF)
    by_owner(nrm[rows:3 * rows], nt)
    gall[0:rows] = cot[0]

    drained = 0
    for k in range(len(pieces)):
        from_x(k)
        if k == 1:
            begin_skip()
        if k >= 2:
            from_y(drained)
            drained += 1
    for k in range(drained, first):
        from_y(k)

    from_mate(0)
    for k in range(first):
        from_core(k)
    stored = mm(nrm[rows:3 * rows], wqf[...].reshape(width, 3 * width))
    proj[rows:3 * rows] = stored.astype(BF)
    for k in range(max(drained, first), len(pieces)):
        from_y(k)
    from_mate(1)
    for k in range(first, len(pieces)):
        from_core(k)
    w_out = wof[...].reshape(width, width)

    def pair_backward(t, p, weights_f32, dctx):
        row0 = (1 + t) * rows
        at = t * rows
        d2 = stack(dctx[:, p * PAIR:(p + 1) * PAIR])
        d_attn = mm(d2, part(row0, p, 2), 1, 1).astype(BF).astype(F32)
        d_scores = weights_f32 * (
            d_attn - jnp.sum(d_attn * weights_f32, axis=-1, keepdims=True))
        d_scores = (d_scores * HEAD_DIM ** (-0.5)).astype(BF)
        dq = fold(mm(d_scores, part(row0, p, 1)))
        dk = mm(d_scores, stack(part(row0, p, 0)), 0, 0)
        dv = mm(weights_f32.astype(BF), d2, 0, 0)
        for i, x in enumerate((dq, dk, dv)):
            dproj[at:at + rows, i * width + p * PAIR:i * width + (p + 1) * PAIR] = x.astype(BF)

    def context_of(row0, p, weights_f32):
        return fold(mm(weights_f32.astype(BF), part(row0, p, 2))).astype(BF)

    def input_cotangent(t, g):
        d_norm = mm(dproj[t * rows:(t + 1) * rows], wqf[...].reshape(width, 3 * width), 1, 1)
        d_norm = d_norm.astype(BF).astype(F32)
        normal, scale = stats(stash[0, t])
        mean = jnp.mean(d_norm, axis=-1, keepdims=True)
        along = jnp.mean(d_norm * normal, axis=-1, keepdims=True)
        return (g.astype(F32) + scale * (d_norm - mean - normal * along)).astype(BF)

    def forward(u):
        outs = [context_of(0, p, softmax(0, p)) for p in range(PAIRS)]
        return (u.astype(F32) + mm(jnp.concatenate(outs, axis=1), w_out)).astype(BF)

    dctx = mm(gall[0:rows], w_out, 1, 1).astype(BF)
    for p in range(PAIRS):
        weights_f32 = softmax(rows, p)
        ctx[0:rows, p * PAIR:(p + 1) * PAIR] = context_of(rows, p, weights_f32)
        pair_backward(0, p, weights_f32, dctx)
    dsend[...] = input_cotangent(0, gall[0:rows])

    def d_copy():
        return remote(dsend, din, rsend.at[0], rrecv.at[0], segment=seg - 1)

    @pl.when(seg > 0)
    def _():
        d_copy().start()

    for p in range(PAIRS):
        weights_f32 = softmax(2 * rows, p)
        prob[p] = weights_f32
        ctx[rows:2 * rows, p * PAIR:(p + 1) * PAIR] = context_of(2 * rows, p, weights_f32)
    by_owner(ctx[...], ct)

    @pl.when(decoder)
    def _():
        skip_copy(0).wait_recv()
        joined[...] = (hid[0].astype(F32) + skin[0].astype(F32)).astype(BF)

    @pl.when(jnp.logical_not(decoder))
    def _():
        joined[...] = hid[0]

    nrm[0:rows] = stats(joined[...])[0].astype(BF)

    proj[0:rows] = mm(nrm[0:rows], wqf[...].reshape(width, 3 * width)).astype(BF)
    ysend[...] = forward(joined[...])

    def y_copy():
        return remote(ysend, yin, rsend.at[1], rrecv.at[1], segment=seg + 1)

    @pl.when(seg < segs - 1)
    def _():
        y_copy().start()

    @pl.when(seg == segs - 1)
    def _():
        gall[rows:2 * rows] = lgrad[0]

    @pl.when(seg < segs - 1)
    def _():
        remote(dsend, din, rsend.at[0], rrecv.at[0], segment=seg + 1).wait_recv()
        gall[rows:2 * rows] = din[...]

    terms = [(o1s, o1r, okeep, o2s, o2r, 0)] + [
        (q1s.at[p], q1r.at[p], qkeep.at[p], q2s.at[p], q2r.at[p], 1 + p) for p in range(PAIRS)]

    def first_hop(term):
        s1, r1, _, _, _, i = term
        return remote(s1, r1, p1s.at[i], p1r.at[i], dp=mate)

    def second_hop(term, off):
        _, _, _, s2, r2, i = term
        return remote(s2.at[peer(off)], r2.at[chip], p2s.at[i, off], p2r.at[i, chip],
                      dp=peer(off) * 2 + core)

    def open_term(term, left, right):
        s1, keep = term[0], term[2]
        s1[...] = mm(left[other], right).astype(BF).reshape(s1.shape)
        first_hop(term).start()
        keep[...] = mm(left[core], right).reshape(keep.shape)

    def pass_term(term):
        _, r1, keep, s2, _, _ = term
        first_hop(term).wait_recv()
        keep[...] = keep[...] + r1[...].astype(F32)
        s2[...] = keep[...].astype(BF)
        for off in range(1, half):
            second_hop(term, off).start()

    def close_term(term):
        _, _, keep, s2, r2, i = term
        total = keep[chip]
        for off in range(1, half):
            src = peer(off)
            remote(s2.at[src], r2.at[src], p2s.at[i, off], p2r.at[i, src],
                   dp=src * 2 + core).wait_recv()
            total = total + r2[src].astype(F32)
        return total

    open_term(terms[0], ct, gall[...])
    dctx = mm(gall[rows:2 * rows], w_out, 1, 1).astype(BF)
    for p in range(PAIRS):
        pair_backward(1, p, prob[p], dctx)
        cols = [dproj[:, i * width + p * PAIR:i * width + (p + 1) * PAIR] for i in range(3)]
        open_term(terms[1 + p], nt, jnp.concatenate(cols, axis=1))
        pass_term(terms[p])
    grads[0] = input_cotangent(1, gall[rows:2 * rows])
    pass_term(terms[PAIRS])

    @pl.when(seg == 0)
    def _():
        joined[...] = ent[0]

    @pl.when(seg > 0)
    def _():
        remote(ysend, yin, rsend.at[1], rrecv.at[1], segment=seg - 1).wait_recv()

    @pl.when(jnp.logical_and(seg > 0, jnp.logical_not(decoder)))
    def _():
        joined[...] = yin[...]

    @pl.when(decoder)
    def _():
        skip_copy(1).wait_recv()
        joined[...] = (yin[...].astype(F32) + skin[1].astype(F32)).astype(BF)

    nrm[0:rows] = stats(joined[...])[0].astype(BF)
    proj[0:rows] = mm(nrm[0:rows], wqf[...].reshape(width, 3 * width)).astype(BF)
    acts[0] = forward(joined[...])

    go[0] = close_term(terms[0])
    for p in range(PAIRS):
        total = close_term(terms[1 + p])
        for i in range(3):
            gq[0, :, i * width + p * PAIR:i * width + (p + 1) * PAIR] = (
                total[:, i * PAIR:(i + 1) * PAIR])

    for copy in sent:
        copy.wait_send()
    for term in terms:
        first_hop(term).wait_send()
        for off in range(1, half):
            second_hop(term, off).wait_send()

    @pl.when(jnp.logical_not(decoder))
    def _():
        for t in range(2):
            skip_copy(t).wait_send()

    @pl.when(seg > 0)
    def _():
        d_copy().wait_send()

    @pl.when(seg < segs - 1)
    def _():
        y_copy().wait_send()


def solution(mesh):
    n, segs = mesh.shape["dp"], mesh.shape["segment"]
    half = n // 2
    in_specs = (
        P("segment", ("groups", "dp"), None),
        P("segment", None, ("groups", "dp"), None),
        P("segment", None, ("groups", "dp"), None),
        P("segment", ("groups", "dp"), None),
        P(None, ("groups", "dp"), None),
        P(None, ("groups", "dp"), None),
        P("segment", "dp", None),
        P("segment", "dp", None),
        P("segment", ("groups", "dp")),
    )
    out_specs = (
        P("segment", ("groups", "dp"), None),
        P("segment", ("groups", "dp"), None),
        P(("groups", "segment"), "dp", None),
        P(("groups", "segment"), "dp", None),
    )

    def step(hidden, stash, skip_store, cotan, entry, loss_grad, wqkv, wout, region):
        rows, width = hidden.shape[1:]
        depth = wqkv.shape[1]
        count = depth // 32 + -(-depth // 64)
        vmem, dma = pltpu.VMEM, pltpu.SemaphoreType.DMA
        block = vmem((rows, width), BF)

        def sums(lead, cols, kind):
            return vmem(lead + (half, depth, cols), kind)

        kinds = (BF, BF, F32, BF, BF)
        outs = pl.pallas_call(
            functools.partial(kernel, n, segs),
            out_shape=(
                vmem(hidden.shape, BF), vmem(hidden.shape, BF),
                vmem(wqkv.shape, F32), vmem(wout.shape, F32),
            ),
            in_specs=[pl.BlockSpec(memory_space=pltpu.HBM)] * 9,
            out_specs=[pl.BlockSpec(memory_space=pltpu.VMEM)] * 4,
            scratch_shapes=[
                *[vmem(x.shape, x.dtype)
                  for x in (hidden, stash, cotan, entry, loss_grad, region)], dma((8,)),
                vmem((n, depth, 3 * width), BF), vmem((n, depth, width), BF),
                vmem((2, rows, width), BF), block, block, block, block, block,
                vmem((2 * rows, width), BF), vmem((3 * rows, width), BF),
                vmem((3 * rows, 3 * width), BF),
                vmem((2, half * depth, 2 * rows), BF), vmem((2, half * depth, 2 * rows), BF),
                vmem((2 * rows, 3 * width), BF), vmem((2 * rows, width), BF),
                vmem((PAIRS, 2 * rows, rows), F32), vmem((2 * rows, rows), F32),
                *[sums((PAIRS,), 3 * PAIR, kind) for kind in kinds],
                *[sums((), width, kind) for kind in kinds],
                *[dma((half, count))] * 8, dma((2,)), dma((2,)), dma((2,)), dma((2,)), dma((2,)), dma((2,)),
                dma((PAIRS + 1,)), dma((PAIRS + 1,)),
                dma((PAIRS + 1, half)), dma((PAIRS + 1, half)), pltpu.SemaphoreType.REGULAR,
            ],
            compiler_params=pltpu.CompilerParams(
                collective_id=0, has_side_effects=True, vmem_limit_bytes=40 << 20),
        )(*[pltpu.with_memory_space_constraint(x, pltpu.HBM) for x in (
            hidden, stash, skip_store, cotan, entry, loss_grad, wqkv, wout, region)])
        return pl.pallas_call(
            flush,
            out_shape=tuple(jax.ShapeDtypeStruct(x.shape, x.dtype) for x in outs),
            in_specs=[pl.BlockSpec(memory_space=pltpu.VMEM)] * 4,
            out_specs=[pl.BlockSpec(memory_space=pltpu.HBM)] * 4,
            scratch_shapes=[dma((4,))],
            compiler_params=pltpu.CompilerParams(vmem_limit_bytes=16 << 20),
        )(*outs)

    return jax.shard_map(
        step, mesh=mesh, in_specs=in_specs, out_specs=out_specs, check_vma=False
    )
```

```python
import functools

import jax
import jax.numpy as jnp
from jax import lax
from jax.experimental import pallas as pl
from jax.experimental.pallas import tpu as pltpu
from jax.sharding import PartitionSpec as P

HEADS = 8
HEAD_DIM = 64
WINDOW = 144
PAIR = 2 * HEAD_DIM
PAIRS = HEADS // 2
BF = jnp.bfloat16
F32 = jnp.float32
MESH = pl.DeviceIdType.MESH


def mm(a, b, ca=1, cb=0):
    return lax.dot_general(a, b, (((ca,), (cb,)), ((), ())), preferred_element_type=F32)


def stats(u):
    up = u.astype(F32)
    centred = up - jnp.mean(up, axis=-1, keepdims=True)
    scale = lax.rsqrt(jnp.mean(centred * centred, axis=-1, keepdims=True) + 1e-05)
    return centred * scale, scale


def flush(*refs):
    srcs, dsts, sems = refs[0:4], refs[4:8], refs[8]
    stores = [pltpu.make_async_copy(srcs[i], dsts[i], sems.at[i]) for i in range(4)]
    for store in stores:
        store.start()
    for store in stores:
        store.wait()


def kernel(n, segs, hid_in, stash_in, skip, cot_in, ent_in, lgrad_in, wq, wo, reg_in,
           acts, grads, gq, go,
           hid, stash, ent, gall, regs, lsem,
           wqf, wof, skin, yin, ysend, dsend, joined, nrm, nrmf, proj, projf, nt, ct, dproj, ctx,
           prob, same2, norm32, scales,
           q1s, q1r, qkeep, o1s, o1r, okeep,
           xs, xr, ys, yr, cs, cr, es, er, wxs, wxr, wcs, wcr, ms, mr, vs, vr,
           ksend, krecv, dss, dsr, ysem, p1s, p1r, ready):
    rows, width = hid_in.shape[1], hid_in.shape[2]
    half = n // 2
    depth = wq.shape[1]
    me = lax.axis_index("dp")
    seg = lax.axis_index("segment")
    grp = lax.axis_index("groups")
    chip, core = me // 2, me % 2
    other = 1 - core
    mate = chip * 2 + other
    mirror = segs - 1 - seg
    encoder = seg < segs // 2
    decoder = seg >= segs // 2
    last = seg == segs - 1

    def peer(off):
        return lax.rem(chip + off, half)

    loads = [pltpu.make_async_copy(src, dst, lsem.at[i]) for i, (src, dst) in enumerate((
        (stash_in.at[0], stash.at[0]), (cot_in.at[0], gall.at[0, 0]), (reg_in, regs[0]),
        (wq.at[0], wqf.at[me]), (wo.at[0], wof.at[me]), (hid_in.at[0], hid), (ent_in.at[0], ent)))]
    for load in loads:
        load.start()
    own_loss = pltpu.make_async_copy(lgrad_in.at[0], gall.at[0, 1], lsem.at[len(loads)])

    @pl.when(last)
    def _():
        own_loss.start()

    barrier = pltpu.get_barrier_semaphore()

    def greet(**where):
        pl.semaphore_signal(barrier, inc=1, device_id=where, device_id_type=MESH)

    greet(groups=1 - grp)
    for off in range(1, half):
        greet(dp=peer(off) * 2 + core)

    @pl.when(seg > 0)
    def _():
        greet(segment=seg - 1)

    @pl.when(seg < segs - 1)
    def _():
        greet(segment=seg + 1)

    greet(dp=mate)
    count = half + 1 + jnp.where(seg > 0, 1, 0)
    pl.semaphore_wait(barrier, count + jnp.where(seg < segs - 1, 1, 0))

    def remote(src, dst, ssem, rsem, **where):
        return pltpu.make_async_remote_copy(
            src_ref=src, dst_ref=dst, send_sem=ssem, recv_sem=rsem,
            device_id=where, device_id_type=MESH)

    sent = []

    def send(copy):
        copy.start()
        sent.append(copy)

    span = depth // 2
    size = 16
    pieces = range(span // size)
    parts = range(2)
    wspan = depth // 2

    def wq_rows(ref, lead, k, group):
        return ref.at[lead, pl.ds(pl.multiple_of(group * span + k * size, size), size)]

    def wo_rows(ref, lead, k):
        return ref.at[lead, pl.ds(k * wspan, wspan)]

    for k in pieces:
        for off in range(1, half):
            send(remote(wq_rows(wq, 0, k, grp), wq_rows(wqf, me, k, grp),
                        xs.at[off, k], xr.at[chip, k], dp=peer(off) * 2 + core))
    for k in parts:
        for off in range(1, half):
            send(remote(wo_rows(wo, 0, k), wo_rows(wof, me, k),
                        wxs.at[off, k], wxr.at[chip, k], dp=peer(off) * 2 + core))
    send(remote(wq.at[0], wqf.at[me], ms.at[0], mr.at[0], dp=mate))
    send(remote(wo.at[0], wof.at[me], ms.at[1], mr.at[1], dp=mate))

    def pass_on(k, off, group, ssem, rsem, **where):
        block = wq_rows(wqf, peer(off) * 2 + core, k, group)
        return remote(block, block, ssem.at[peer(off), k], rsem.at[peer(off), k], **where)

    def from_x(k):
        for off in range(1, half):
            pass_on(k, off, grp, xs, xr, dp=mate).wait_recv()
            send(pass_on(k, off, grp, ys, yr, groups=1 - grp))
            send(pass_on(k, off, grp, cs, cr, dp=mate))

    def from_y(k):
        for off in range(1, half):
            pass_on(k, off, 1 - grp, ys, yr, groups=1 - grp).wait_recv()
            send(pass_on(k, off, 1 - grp, es, er, dp=mate))

    def wo_from_x(k):
        for off in range(1, half):
            block = wo_rows(wof, peer(off) * 2 + core, k)
            remote(block, block, wxs.at[off, k], wxr.at[peer(off), k], dp=mate).wait_recv()
            send(remote(block, block, wcs.at[peer(off), k], wcr.at[peer(off), k], dp=mate))

    def from_core():
        for k in pieces:
            for off in range(1, half):
                for group, rsem in ((grp, cr), (1 - grp, er)):
                    block = wq_rows(wqf, peer(off) * 2 + other, k, group)
                    remote(block, block, cs.at[peer(off), k], rsem.at[peer(off), k],
                           dp=mate).wait_recv()

    def wo_from_core():
        for k in parts:
            for off in range(1, half):
                block = wo_rows(wof, peer(off) * 2 + other, k)
                remote(block, block, wcs.at[peer(off), k], wcr.at[peer(off), k],
                       dp=mate).wait_recv()

    def from_mate(w, ref):
        remote(ref.at[mate], ref.at[mate], ms.at[w], mr.at[w], dp=mate).wait_recv()

    def window_copies(off):
        return [remote(src, dst, vs.at[off, i], vr.at[off, i], dp=peer(off) * 2 + core)
                for i, (src, dst) in enumerate((
                    (stash_in.at[0, 0], stash.at[off, 0]), (cot_in.at[0], gall.at[off, 0]),
                    (reg_in, regs[off]), (stash_in.at[0, 1], stash.at[off, 1])))]

    def loss_copy(off):
        return remote(lgrad_in.at[0], gall.at[off, 1], vs.at[off, 4], vr.at[off, 4],
                      dp=peer(off) * 2 + core)

    def send_windows():
        for off in range(1, half):
            for copy in window_copies(off):
                send(copy)

            @pl.when(last)
            def _():
                loss_copy(off).start()

    def skip_copy(t):
        return remote(skip.at[0, t], skin.at[t], ksend.at[t], krecv.at[t], segment=mirror)

    def announce():
        pl.semaphore_signal(ready, inc=1, device_id={"segment": seg - 1}, device_id_type=MESH)

    def chain(here):
        @pl.when(here)
        def _():
            pl.semaphore_wait(ready, 1)

        @pl.when(jnp.logical_and(here, seg > 0))
        def _():
            announce()

    near = seg == segs // 2 - 1

    @pl.when(near)
    def _():
        skip_copy(0).start()

    if segs > 2:
        @pl.when(seg == segs - 2)
        def _():
            announce()

    for load in loads[:3]:
        load.wait()

    lane = lax.broadcasted_iota(jnp.int32, (rows, PAIR), 1) < HEAD_DIM
    lo = lane.astype(F32).astype(BF)
    hi = (1.0 - lane.astype(F32)).astype(BF)

    def masks(j):
        labels = jnp.broadcast_to(regs[j][...], (16, rows))
        onehot = (lax.broadcasted_iota(jnp.int32, (16, rows), 0) == labels).astype(F32).astype(BF)
        same = mm(onehot, onehot, 0, 0)
        same2[j, 0:rows] = same
        same2[j, rows:2 * rows] = same

    def at(t, j):
        return (j * 2 + t) * rows

    def stack(x):
        return jnp.concatenate([x * lo, x * hi], axis=0)

    def fold(x):
        return jnp.where(lane, x[:rows], x[rows:])

    def part(ref, r, p, which):
        return ref[r:r + rows, which * width + p * PAIR:which * width + (p + 1) * PAIR]

    def softmax(ref, r, p, j):
        scores = mm(stack(part(ref, r, p, 0)), part(ref, r, p, 1), 1, 1) * HEAD_DIM ** (-0.5)
        scores = jnp.where(same2[j] > 0.5, scores, F32(-1000000000.0))
        e = jnp.exp(scores - jnp.max(scores, axis=-1, keepdims=True))
        return e * (1.0 / jnp.sum(e, axis=-1, keepdims=True))

    masks(0)
    for t in range(2):
        normal, scale = stats(stash[0, t])
        norm32[t] = normal
        scales[t] = jnp.broadcast_to(scale, (rows, 128))
        nrm[at(t, 0):at(t, 0) + rows] = normal.astype(BF)

    chain(seg == segs - 3)
    from_x(0)
    chain(seg < segs - 3)

    @pl.when(jnp.logical_and(encoder, seg < segs // 2 - 1))
    def _():
        skip_copy(0).start()

    for k in pieces[1:]:
        from_x(k)
    send_windows()
    for load in loads[3:]:
        load.wait()
    middle = len(pieces) // 2
    for k in pieces[:middle]:
        from_y(k)
    wo_from_x(0)
    for k in pieces[middle:-1]:
        from_y(k)
    wo_from_x(1)
    for k in pieces[-1:]:
        from_y(k)

    @pl.when(encoder)
    def _():
        skip_copy(1).start()

    from_mate(0, wqf)
    from_core()

    def w_qkv():
        return wqf[...].reshape(width, 3 * width)

    def w_out():
        return wof[...].reshape(width, width)

    proj[0:2 * rows] = mm(nrm[0:2 * rows], w_qkv()).astype(BF)
    from_mate(1, wof)
    wo_from_core()

    def pair_backward(t, j, p, weights_f32, dctx):
        r = at(t, j)
        d2 = stack(dctx[:, p * PAIR:(p + 1) * PAIR])
        d_attn = mm(d2, part(proj, r, p, 2), 1, 1).astype(BF).astype(F32)
        d_scores = weights_f32 * (
            d_attn - jnp.sum(d_attn * weights_f32, axis=-1, keepdims=True))
        d_scores = (d_scores * HEAD_DIM ** (-0.5)).astype(BF)
        dq = fold(mm(d_scores, part(proj, r, p, 1)))
        dk = mm(d_scores, stack(part(proj, r, p, 0)), 0, 0)
        dv = mm(weights_f32.astype(BF), d2, 0, 0)
        for i, x in enumerate((dq, dk, dv)):
            dproj[r:r + rows, i * width + p * PAIR:i * width + (p + 1) * PAIR] = x.astype(BF)

    def context_of(ref, r, p, weights_f32):
        return fold(mm(weights_f32.astype(BF), part(ref, r, p, 2))).astype(BF)

    def input_cotangent(t):
        r = at(t, 0)
        d_norm = mm(dproj[r:r + rows], w_qkv(), 1, 1).astype(BF).astype(F32)
        normal, scale = norm32[t], scales[t][:, 0:1]
        mean = jnp.mean(d_norm, axis=-1, keepdims=True)
        along = jnp.mean(d_norm * normal, axis=-1, keepdims=True)
        return (gall[0, t].astype(F32) + scale * (d_norm - mean - normal * along)).astype(BF)

    def forward(u):
        nrmf[...] = stats(u)[0].astype(BF)
        projf[...] = mm(nrmf[...], w_qkv()).astype(BF)
        outs = [context_of(projf, 0, p, softmax(projf, 0, p, 0)) for p in range(PAIRS)]
        return (u.astype(F32) + mm(jnp.concatenate(outs, axis=1), w_out())).astype(BF)

    def d_ctx(t, j):
        return mm(gall[j, t], w_out(), 1, 1).astype(BF)

    def attend(t, j, p):
        r = at(t, j)
        weights_f32 = softmax(proj, r, p, j)
        ctx[r:r + rows, p * PAIR:(p + 1) * PAIR] = context_of(proj, r, p, weights_f32)
        return weights_f32

    dctx = d_ctx(0, 0)
    for p in range(PAIRS):
        pair_backward(0, 0, p, attend(0, 0, p), dctx)
    dsend[...] = input_cotangent(0)

    def d_copy(off):
        return remote(dsend, gall.at[off, 1], dss.at[off], dsr.at[off],
                      segment=seg - 1, dp=peer(off) * 2 + core)

    @pl.when(seg > 0)
    def _():
        for off in range(half):
            d_copy(off).start()

    @pl.when(decoder)
    def _():
        skip_copy(0).wait_recv()
        joined[...] = (hid[...].astype(F32) + skin[0].astype(F32)).astype(BF)

    @pl.when(encoder)
    def _():
        joined[...] = hid[...]

    ysend[...] = forward(joined[...])

    def y_copy():
        return remote(ysend, yin, ysem.at[0], ysem.at[1], segment=seg + 1)

    @pl.when(seg < segs - 1)
    def _():
        y_copy().start()

    for j in range(1, half):
        for copy in window_copies(j):
            copy.wait_recv()
        masks(j)
        for t in range(2):
            nrm[at(t, j):at(t, j) + rows] = stats(stash[j, t])[0].astype(BF)
    if half > 1:
        proj[2 * rows:] = mm(nrm[2 * rows:], w_qkv()).astype(BF)
    for j in range(1, half):
        dctx = d_ctx(0, j)
        for p in range(PAIRS):
            pair_backward(0, j, p, attend(0, j, p), dctx)
    for j in range(half):
        for p in range(PAIRS):
            prob[j, p] = attend(1, j, p)

    def by_owner(src, dest):
        block = src[:, pl.ds(pl.multiple_of(chip * 2 * depth, 2 * depth), 2 * depth)]
        dest[...] = block.T.reshape(dest.shape)

    by_owner(nrm, nt)
    by_owner(ctx, ct)

    def cotangent_arrives(j):
        @pl.when(seg < segs - 1)
        def _():
            d_copy(j).wait_recv()

        @pl.when(last)
        def _():
            if j == 0:
                own_loss.wait()
            else:
                loss_copy(j).wait_recv()

    terms = [(o1s, o1r, okeep, 0)] + [
        (q1s.at[p], q1r.at[p], qkeep.at[p], 1 + p) for p in range(PAIRS)]

    def hop(term):
        s1, r1, _, i = term
        return remote(s1, r1, p1s.at[i], p1r.at[i], dp=mate)

    def open_term(term, left, right):
        s1, _, keep, _ = term
        s1[...] = mm(left[other], right).astype(BF)
        hop(term).start()
        keep[...] = mm(left[core], right)

    cotangent_arrives(0)
    dctx = d_ctx(1, 0)
    for p in range(PAIRS):
        pair_backward(1, 0, p, prob[0, p], dctx)
    grads[0] = input_cotangent(1)
    for j in range(1, half):
        cotangent_arrives(j)
    open_term(terms[0], ct, gall[...].reshape(2 * half * rows, width))
    dctxs = [d_ctx(1, j) for j in range(1, half)]
    for p in range(PAIRS):
        for j in range(1, half):
            pair_backward(1, j, p, prob[j, p], dctxs[j - 1])
        cols = [dproj[:, i * width + p * PAIR:i * width + (p + 1) * PAIR] for i in range(3)]
        open_term(terms[1 + p], nt, jnp.concatenate(cols, axis=1))

    @pl.when(seg == 0)
    def _():
        joined[...] = ent[...]

    @pl.when(seg > 0)
    def _():
        y_copy().wait_recv()

    @pl.when(jnp.logical_and(seg > 0, encoder))
    def _():
        joined[...] = yin[...]

    @pl.when(decoder)
    def _():
        skip_copy(1).wait_recv()
        joined[...] = (yin[...].astype(F32) + skin[1].astype(F32)).astype(BF)

    acts[0] = forward(joined[...])

    def close_term(term):
        hop(term).wait_recv()
        return term[2][...] + term[1][...].astype(F32)

    go[0] = close_term(terms[0])
    for p in range(PAIRS):
        total = close_term(terms[1 + p])
        for i in range(3):
            gq[0, :, i * width + p * PAIR:i * width + (p + 1) * PAIR] = (
                total[:, i * PAIR:(i + 1) * PAIR])

    for copy in sent:
        copy.wait_send()
    for term in terms:
        hop(term).wait_send()

    @pl.when(last)
    def _():
        for off in range(1, half):
            loss_copy(off).wait_send()

    @pl.when(encoder)
    def _():
        for t in range(2):
            skip_copy(t).wait_send()

    @pl.when(seg > 0)
    def _():
        for off in range(half):
            d_copy(off).wait_send()

    @pl.when(seg < segs - 1)
    def _():
        y_copy().wait_send()


def solution(mesh):
    n, segs = mesh.shape["dp"], mesh.shape["segment"]
    half = n // 2
    in_specs = (
        P("segment", ("groups", "dp"), None),
        P("segment", None, ("groups", "dp"), None),
        P("segment", None, ("groups", "dp"), None),
        P("segment", ("groups", "dp"), None),
        P(None, ("groups", "dp"), None),
        P(None, ("groups", "dp"), None),
        P("segment", "dp", None),
        P("segment", "dp", None),
        P("segment", ("groups", "dp")),
    )
    out_specs = (
        P("segment", ("groups", "dp"), None),
        P("segment", ("groups", "dp"), None),
        P(("groups", "segment"), "dp", None),
        P(("groups", "segment"), "dp", None),
    )

    def step(hidden, stash, skip_store, cotan, entry, loss_grad, wqkv, wout, region):
        rows, width = hidden.shape[1:]
        depth = wqkv.shape[1]
        pieces = depth // 32
        vmem, dma = pltpu.VMEM, pltpu.SemaphoreType.DMA
        block = vmem((rows, width), BF)
        windows = 2 * half * rows

        outs = pl.pallas_call(
            functools.partial(kernel, n, segs),
            out_shape=(
                vmem(hidden.shape, BF), vmem(hidden.shape, BF),
                vmem(wqkv.shape, F32), vmem(wout.shape, F32),
            ),
            in_specs=[pl.BlockSpec(memory_space=pltpu.HBM)] * 9,
            out_specs=[pl.BlockSpec(memory_space=pltpu.VMEM)] * 4,
            scratch_shapes=[
                block, vmem((half, 2, rows, width), BF), block, vmem((half, 2, rows, width), BF),
                [vmem(region.shape, region.dtype) for _ in range(half)], dma((8,)),
                vmem((n, depth, 3 * width), BF), vmem((n, depth, width), BF),
                vmem((2, rows, width), BF), block, block, block, block,
                vmem((windows, width), BF), block,
                vmem((windows, 3 * width), BF), vmem((rows, 3 * width), BF),
                vmem((2, depth, windows), BF), vmem((2, depth, windows), BF),
                vmem((windows, 3 * width), BF), vmem((windows, width), BF),
                vmem((half, PAIRS, 2 * rows, rows), F32), vmem((half, 2 * rows, rows), F32),
                vmem((2, rows, width), F32), vmem((2, rows, 128), F32),
                *[vmem((PAIRS, depth, 3 * PAIR), kind) for kind in (BF, BF, F32)],
                *[vmem((depth, width), kind) for kind in (BF, BF, F32)],
                *[dma((half, pieces))] * 8, *[dma((half, 2))] * 4, dma((2,)), dma((2,)),
                dma((half, 5)), dma((half, 5)), dma((2,)), dma((2,)),
                dma((half,)), dma((half,)), dma((2,)),
                dma((PAIRS + 1,)), dma((PAIRS + 1,)), pltpu.SemaphoreType.REGULAR,
            ],
            compiler_params=pltpu.CompilerParams(
                collective_id=0, has_side_effects=True, vmem_limit_bytes=40 << 20),
        )(*[pltpu.with_memory_space_constraint(x, pltpu.HBM) for x in (
            hidden, stash, skip_store, cotan, entry, loss_grad, wqkv, wout, region)])
        return pl.pallas_call(
            flush,
            out_shape=tuple(jax.ShapeDtypeStruct(x.shape, x.dtype) for x in outs),
            in_specs=[pl.BlockSpec(memory_space=pltpu.VMEM)] * 4,
            out_specs=[pl.BlockSpec(memory_space=pltpu.HBM)] * 4,
            scratch_shapes=[dma((4,))],
            compiler_params=pltpu.CompilerParams(vmem_limit_bytes=16 << 20),
        )(*outs)

    return jax.shard_map(
        step, mesh=mesh, in_specs=in_specs, out_specs=out_specs, check_vma=False
    )
```

```python
import functools

import jax
import jax.numpy as jnp
from jax import lax
from jax.experimental import pallas as pl
from jax.experimental.pallas import tpu as pltpu
from jax.sharding import PartitionSpec as P

HEADS = 8
HEAD_DIM = 64
WINDOW = 144
QUAD = 4 * HEAD_DIM
QUADS = HEADS // 4
BF = jnp.bfloat16
F32 = jnp.float32
MESH = pl.DeviceIdType.MESH


def mm(a, b, ca=1, cb=0):
    return lax.dot_general(a, b, (((ca,), (cb,)), ((), ())), preferred_element_type=F32)


def stats(u):
    up = u.astype(F32)
    centred = up - jnp.mean(up, axis=-1, keepdims=True)
    scale = lax.rsqrt(jnp.mean(centred * centred, axis=-1, keepdims=True) + 1e-05)
    return centred * scale, scale


def flush(*refs):
    srcs, dsts, sems = refs[0:4], refs[4:8], refs[8]
    stores = [pltpu.make_async_copy(srcs[i], dsts[i], sems.at[i]) for i in range(4)]
    for store in stores:
        store.start()
    for store in stores:
        store.wait()


def kernel(n, segs, hid_in, stash_in, skip, cot_in, ent_in, lgrad_in, wq, wo, reg_in,
           acts, grads, gq, go,
           hid, stash, ent, gall, regs, lsem,
           wqf, wof, skin, yin, ysend, dsend, joined, nrm, nrmf, proj, projf, nt, ct, dproj, ctx,
           prob, same4, norm32, scales,
           q1s, q1r, qkeep, o1s, o1r, okeep,
           xs, xr, ys, yr, cs, cr, es, er, wxs, wxr, wcs, wcr, ms, mr, vs, vr,
           ksend, krecv, dss, dsr, ysem, p1s, p1r, ready):
    rows, width = hid_in.shape[1], hid_in.shape[2]
    half = n // 2
    depth = wq.shape[1]
    me = lax.axis_index("dp")
    seg = lax.axis_index("segment")
    grp = lax.axis_index("groups")
    chip, core = me // 2, me % 2
    other = 1 - core
    mate = chip * 2 + other
    mirror = segs - 1 - seg
    encoder = seg < segs // 2
    decoder = seg >= segs // 2
    last = seg == segs - 1

    def peer(off):
        return lax.rem(chip + off, half)

    loads = [pltpu.make_async_copy(src, dst, lsem.at[i]) for i, (src, dst) in enumerate((
        (stash_in.at[0], stash.at[0]), (cot_in.at[0], gall.at[0, 0]), (reg_in, regs[0]),
        (wq.at[0], wqf.at[me]), (wo.at[0], wof.at[me]), (hid_in.at[0], hid), (ent_in.at[0], ent)))]
    for load in loads:
        load.start()
    own_loss = pltpu.make_async_copy(lgrad_in.at[0], gall.at[0, 1], lsem.at[len(loads)])

    @pl.when(last)
    def _():
        own_loss.start()

    barrier = pltpu.get_barrier_semaphore()

    def greet(**where):
        pl.semaphore_signal(barrier, inc=1, device_id=where, device_id_type=MESH)

    greet(groups=1 - grp)
    for off in range(1, half):
        greet(dp=peer(off) * 2 + core)

    @pl.when(seg > 0)
    def _():
        greet(segment=seg - 1)

    @pl.when(seg < segs - 1)
    def _():
        greet(segment=seg + 1)

    greet(dp=mate)
    count = half + 1 + jnp.where(seg > 0, 1, 0)
    pl.semaphore_wait(barrier, count + jnp.where(seg < segs - 1, 1, 0))

    def remote(src, dst, ssem, rsem, **where):
        return pltpu.make_async_remote_copy(
            src_ref=src, dst_ref=dst, send_sem=ssem, recv_sem=rsem,
            device_id=where, device_id_type=MESH)

    sent = []

    def send(copy):
        copy.start()
        sent.append(copy)

    span = depth // 2
    size = 16
    pieces = range(span // size)
    parts = range(2)
    wspan = depth // 2

    def wq_rows(ref, lead, k, group):
        return ref.at[lead, pl.ds(pl.multiple_of(group * span + k * size, size), size)]

    def wo_rows(ref, lead, k):
        return ref.at[lead, pl.ds(k * wspan, wspan)]

    for k in pieces:
        for off in range(1, half):
            send(remote(wq_rows(wq, 0, k, grp), wq_rows(wqf, me, k, grp),
                        xs.at[off, k], xr.at[chip, k], dp=peer(off) * 2 + core))
    for k in parts:
        for off in range(1, half):
            send(remote(wo_rows(wo, 0, k), wo_rows(wof, me, k),
                        wxs.at[off, k], wxr.at[chip, k], dp=peer(off) * 2 + core))
    send(remote(wq.at[0], wqf.at[me], ms.at[0], mr.at[0], dp=mate))
    send(remote(wo.at[0], wof.at[me], ms.at[1], mr.at[1], dp=mate))

    def pass_on(k, off, group, ssem, rsem, **where):
        block = wq_rows(wqf, peer(off) * 2 + core, k, group)
        return remote(block, block, ssem.at[peer(off), k], rsem.at[peer(off), k], **where)

    def from_x(k):
        for off in range(1, half):
            pass_on(k, off, grp, xs, xr, dp=mate).wait_recv()
            send(pass_on(k, off, grp, ys, yr, groups=1 - grp))
            send(pass_on(k, off, grp, cs, cr, dp=mate))

    def from_y(k):
        for off in range(1, half):
            pass_on(k, off, 1 - grp, ys, yr, groups=1 - grp).wait_recv()
            send(pass_on(k, off, 1 - grp, es, er, dp=mate))

    def wo_from_x(k):
        for off in range(1, half):
            block = wo_rows(wof, peer(off) * 2 + core, k)
            remote(block, block, wxs.at[off, k], wxr.at[peer(off), k], dp=mate).wait_recv()
            send(remote(block, block, wcs.at[peer(off), k], wcr.at[peer(off), k], dp=mate))

    def from_core():
        for k in pieces:
            for off in range(1, half):
                for group, rsem in ((grp, cr), (1 - grp, er)):
                    block = wq_rows(wqf, peer(off) * 2 + other, k, group)
                    remote(block, block, cs.at[peer(off), k], rsem.at[peer(off), k],
                           dp=mate).wait_recv()

    def wo_from_core():
        for k in parts:
            for off in range(1, half):
                block = wo_rows(wof, peer(off) * 2 + other, k)
                remote(block, block, wcs.at[peer(off), k], wcr.at[peer(off), k],
                       dp=mate).wait_recv()

    def from_mate(w, ref):
        remote(ref.at[mate], ref.at[mate], ms.at[w], mr.at[w], dp=mate).wait_recv()

    def window_copies(off):
        return [remote(src, dst, vs.at[off, i], vr.at[off, i], dp=peer(off) * 2 + core)
                for i, (src, dst) in enumerate((
                    (stash_in.at[0, 0], stash.at[off, 0]), (cot_in.at[0], gall.at[off, 0]),
                    (reg_in, regs[off]), (stash_in.at[0, 1], stash.at[off, 1])))]

    def loss_copy(off):
        return remote(lgrad_in.at[0], gall.at[off, 1], vs.at[off, 4], vr.at[off, 4],
                      dp=peer(off) * 2 + core)

    def send_windows():
        for off in range(1, half):
            for copy in window_copies(off):
                send(copy)

            @pl.when(last)
            def _():
                loss_copy(off).start()

    def skip_copy(t):
        return remote(skip.at[0, t], skin.at[t], ksend.at[t], krecv.at[t], segment=mirror)

    def announce():
        pl.semaphore_signal(ready, inc=1, device_id={"segment": seg - 1}, device_id_type=MESH)

    def chain(here):
        @pl.when(here)
        def _():
            pl.semaphore_wait(ready, 1)

        @pl.when(jnp.logical_and(here, seg > 0))
        def _():
            announce()

    near = seg == segs // 2 - 1

    @pl.when(near)
    def _():
        skip_copy(0).start()

    if segs > 2:
        @pl.when(seg == segs - 2)
        def _():
            announce()

    for load in loads[:3]:
        load.wait()

    scale = HEAD_DIM ** (-0.5)
    lane = lax.broadcasted_iota(jnp.int32, (rows, QUAD), 1)
    heads = [jnp.logical_and(lane >= h * HEAD_DIM, lane < (h + 1) * HEAD_DIM).astype(F32)
             for h in range(4)]
    ones = [h.astype(BF) for h in heads]
    eighths = [(h * scale).astype(BF) for h in heads]
    left = lax.broadcasted_iota(jnp.int32, (rows, QUAD // 2), 1) < HEAD_DIM

    def masks(j):
        labels = jnp.broadcast_to(regs[j][...], (16, rows))
        onehot = (lax.broadcasted_iota(jnp.int32, (16, rows), 0) == labels).astype(F32)
        wide = jnp.concatenate([onehot] * 4, axis=1).astype(BF)
        same4[j] = mm(onehot.astype(BF), wide, 0, 0)

    def at(t, j):
        return (j * 2 + t) * rows

    def stack(x, by):
        return jnp.concatenate([x * h for h in by], axis=0)

    def fold(x):
        return jnp.concatenate(
            [jnp.where(left, x[2 * i * rows:(2 * i + 1) * rows, i * QUAD // 2:(i + 1) * QUAD // 2],
                       x[(2 * i + 1) * rows:(2 * i + 2) * rows, i * QUAD // 2:(i + 1) * QUAD // 2])
             for i in range(2)], axis=1)

    def part(ref, r, p, which):
        return ref[r:r + rows, which * width + p * QUAD:which * width + (p + 1) * QUAD]

    def softmax(ref, r, p, j):
        scores = mm(part(ref, r, p, 1), stack(part(ref, r, p, 0), eighths), 1, 1)
        scores = jnp.where(same4[j] > 0.5, scores, F32(-1000000000.0))
        e = jnp.exp(scores - jnp.max(scores, axis=0, keepdims=True))
        return e * (1.0 / jnp.sum(e, axis=0, keepdims=True))

    masks(0)
    for t in range(2):
        normal, inverse = stats(stash[0, t])
        norm32[t] = normal
        scales[t] = jnp.broadcast_to(inverse, (rows, 128))
        nrm[at(t, 0):at(t, 0) + rows] = normal.astype(BF)

    chain(seg == segs - 3)
    from_x(0)
    chain(seg < segs - 3)

    @pl.when(jnp.logical_and(encoder, seg < segs // 2 - 1))
    def _():
        skip_copy(0).start()

    for k in pieces[1:]:
        from_x(k)
    send_windows()
    for load in loads[3:]:
        load.wait()
    middle = len(pieces) // 2
    for k in pieces[:middle]:
        from_y(k)
    wo_from_x(0)
    for k in pieces[middle:-1]:
        from_y(k)
    wo_from_x(1)
    for k in pieces[-1:]:
        from_y(k)

    @pl.when(encoder)
    def _():
        skip_copy(1).start()

    from_mate(0, wqf)
    from_core()

    def w_qkv():
        return wqf[...].reshape(width, 3 * width)

    def w_out():
        return wof[...].reshape(width, width)

    proj[0:2 * rows] = mm(nrm[0:2 * rows], w_qkv()).astype(BF)
    from_mate(1, wof)
    wo_from_core()

    def quad_backward(t, j, p, weights_f32, dctx):
        r = at(t, j)
        d4 = stack(dctx[:, p * QUAD:(p + 1) * QUAD], ones)
        d_attn = mm(part(proj, r, p, 2), d4, 1, 1).astype(BF).astype(F32)
        d_scores = (weights_f32 * (
            d_attn - jnp.sum(d_attn * weights_f32, axis=0, keepdims=True))).astype(BF)
        dq = fold(mm(d_scores, part(proj, r, p, 1), 0, 0)) * scale
        dk = mm(d_scores, stack(part(proj, r, p, 0), eighths))
        dv = mm(weights_f32.astype(BF), d4)
        for i, x in enumerate((dq, dk, dv)):
            dproj[r:r + rows, i * width + p * QUAD:i * width + (p + 1) * QUAD] = x.astype(BF)

    def context_of(ref, r, p, weights_f32):
        return fold(mm(weights_f32.astype(BF), part(ref, r, p, 2), 0, 0)).astype(BF)

    def input_cotangent(t):
        r = at(t, 0)
        d_norm = mm(dproj[r:r + rows], w_qkv(), 1, 1).astype(BF).astype(F32)
        normal, inverse = norm32[t], scales[t][:, 0:1]
        mean = jnp.mean(d_norm, axis=-1, keepdims=True)
        along = jnp.mean(d_norm * normal, axis=-1, keepdims=True)
        return (gall[0, t].astype(F32) + inverse * (d_norm - mean - normal * along)).astype(BF)

    def forward(u):
        nrmf[...] = stats(u)[0].astype(BF)
        projf[...] = mm(nrmf[...], w_qkv()).astype(BF)
        outs = [context_of(projf, 0, p, softmax(projf, 0, p, 0)) for p in range(QUADS)]
        return (u.astype(F32) + mm(jnp.concatenate(outs, axis=1), w_out())).astype(BF)

    def d_ctx(t, j):
        return mm(gall[j, t], w_out(), 1, 1).astype(BF)

    def attend(t, j, p):
        r = at(t, j)
        weights_f32 = softmax(proj, r, p, j)
        ctx[r:r + rows, p * QUAD:(p + 1) * QUAD] = context_of(proj, r, p, weights_f32)
        return weights_f32

    dctx = d_ctx(0, 0)
    for p in range(QUADS):
        quad_backward(0, 0, p, attend(0, 0, p), dctx)
    dsend[...] = input_cotangent(0)

    def d_copy(off):
        return remote(dsend, gall.at[off, 1], dss.at[off], dsr.at[off],
                      segment=seg - 1, dp=peer(off) * 2 + core)

    @pl.when(seg > 0)
    def _():
        for off in range(half):
            d_copy(off).start()

    @pl.when(decoder)
    def _():
        skip_copy(0).wait_recv()
        joined[...] = (hid[...].astype(F32) + skin[0].astype(F32)).astype(BF)

    @pl.when(encoder)
    def _():
        joined[...] = hid[...]

    ysend[...] = forward(joined[...])

    def y_copy():
        return remote(ysend, yin, ysem.at[0], ysem.at[1], segment=seg + 1)

    @pl.when(seg < segs - 1)
    def _():
        y_copy().start()

    for p in range(QUADS):
        prob[0, p] = attend(1, 0, p)

    def peer_window(t, j, copies):
        for copy in copies:
            copy.wait_recv()
        if t == 0:
            masks(j)
        r = at(t, j)
        nrm[r:r + rows] = stats(stash[j, t])[0].astype(BF)
        proj[r:r + rows] = mm(nrm[r:r + rows], w_qkv()).astype(BF)

    for j in range(1, half):
        peer_window(0, j, window_copies(j)[:3])
        dctx = d_ctx(0, j)
        for p in range(QUADS):
            quad_backward(0, j, p, attend(0, j, p), dctx)
    for j in range(1, half):
        peer_window(1, j, window_copies(j)[3:])
        for p in range(QUADS):
            prob[j, p] = attend(1, j, p)

    def by_owner(src, dest):
        block = src[:, pl.ds(pl.multiple_of(chip * 2 * depth, 2 * depth), 2 * depth)]
        dest[...] = block.T.reshape(dest.shape)

    by_owner(nrm, nt)
    by_owner(ctx, ct)

    def cotangent_arrives(j):
        @pl.when(seg < segs - 1)
        def _():
            d_copy(j).wait_recv()

        @pl.when(last)
        def _():
            if j == 0:
                own_loss.wait()
            else:
                loss_copy(j).wait_recv()

    terms = [(o1s, o1r, okeep, 0)] + [
        (q1s.at[p], q1r.at[p], qkeep.at[p], 1 + p) for p in range(QUADS)]

    def hop(term):
        s1, r1, _, i = term
        return remote(s1, r1, p1s.at[i], p1r.at[i], dp=mate)

    def open_term(term, left, right):
        s1, _, keep, _ = term
        s1[...] = mm(left[other], right).astype(BF)
        hop(term).start()
        keep[...] = mm(left[core], right)

    cotangent_arrives(0)
    dctx = d_ctx(1, 0)
    for p in range(QUADS):
        quad_backward(1, 0, p, prob[0, p], dctx)
    grads[0] = input_cotangent(1)
    for j in range(1, half):
        cotangent_arrives(j)
    open_term(terms[0], ct, gall[...].reshape(2 * half * rows, width))
    dctxs = [d_ctx(1, j) for j in range(1, half)]
    for p in range(QUADS):
        for j in range(1, half):
            quad_backward(1, j, p, prob[j, p], dctxs[j - 1])
        cols = [dproj[:, i * width + p * QUAD:i * width + (p + 1) * QUAD] for i in range(3)]
        open_term(terms[1 + p], nt, jnp.concatenate(cols, axis=1))

    @pl.when(seg == 0)
    def _():
        joined[...] = ent[...]

    @pl.when(seg > 0)
    def _():
        y_copy().wait_recv()

    @pl.when(jnp.logical_and(seg > 0, encoder))
    def _():
        joined[...] = yin[...]

    @pl.when(decoder)
    def _():
        skip_copy(1).wait_recv()
        joined[...] = (yin[...].astype(F32) + skin[1].astype(F32)).astype(BF)

    acts[0] = forward(joined[...])

    def close_term(term):
        hop(term).wait_recv()
        return term[2][...] + term[1][...].astype(F32)

    go[0] = close_term(terms[0])
    for p in range(QUADS):
        total = close_term(terms[1 + p])
        for i in range(3):
            gq[0, :, i * width + p * QUAD:i * width + (p + 1) * QUAD] = (
                total[:, i * QUAD:(i + 1) * QUAD])

    for copy in sent:
        copy.wait_send()
    for term in terms:
        hop(term).wait_send()

    @pl.when(last)
    def _():
        for off in range(1, half):
            loss_copy(off).wait_send()

    @pl.when(encoder)
    def _():
        for t in range(2):
            skip_copy(t).wait_send()

    @pl.when(seg > 0)
    def _():
        for off in range(half):
            d_copy(off).wait_send()

    @pl.when(seg < segs - 1)
    def _():
        y_copy().wait_send()


def solution(mesh):
    n, segs = mesh.shape["dp"], mesh.shape["segment"]
    half = n // 2
    in_specs = (
        P("segment", ("groups", "dp"), None),
        P("segment", None, ("groups", "dp"), None),
        P("segment", None, ("groups", "dp"), None),
        P("segment", ("groups", "dp"), None),
        P(None, ("groups", "dp"), None),
        P(None, ("groups", "dp"), None),
        P("segment", "dp", None),
        P("segment", "dp", None),
        P("segment", ("groups", "dp")),
    )
    out_specs = (
        P("segment", ("groups", "dp"), None),
        P("segment", ("groups", "dp"), None),
        P(("groups", "segment"), "dp", None),
        P(("groups", "segment"), "dp", None),
    )

    def step(hidden, stash, skip_store, cotan, entry, loss_grad, wqkv, wout, region):
        rows, width = hidden.shape[1:]
        depth = wqkv.shape[1]
        pieces = depth // 32
        vmem, dma = pltpu.VMEM, pltpu.SemaphoreType.DMA
        block = vmem((rows, width), BF)
        windows = 2 * half * rows

        outs = pl.pallas_call(
            functools.partial(kernel, n, segs),
            out_shape=(
                vmem(hidden.shape, BF), vmem(hidden.shape, BF),
                vmem(wqkv.shape, F32), vmem(wout.shape, F32),
            ),
            in_specs=[pl.BlockSpec(memory_space=pltpu.HBM)] * 9,
            out_specs=[pl.BlockSpec(memory_space=pltpu.VMEM)] * 4,
            scratch_shapes=[
                block, vmem((half, 2, rows, width), BF), block, vmem((half, 2, rows, width), BF),
                [vmem(region.shape, region.dtype) for _ in range(half)], dma((8,)),
                vmem((n, depth, 3 * width), BF), vmem((n, depth, width), BF),
                vmem((2, rows, width), BF), block, block, block, block,
                vmem((windows, width), BF), block,
                vmem((windows, 3 * width), BF), vmem((rows, 3 * width), BF),
                vmem((2, depth, windows), BF), vmem((2, depth, windows), BF),
                vmem((windows, 3 * width), BF), vmem((windows, width), BF),
                vmem((half, QUADS, rows, 4 * rows), F32), vmem((half, rows, 4 * rows), F32),
                vmem((2, rows, width), F32), vmem((2, rows, 128), F32),
                *[vmem((QUADS, depth, 3 * QUAD), kind) for kind in (BF, BF, F32)],
                *[vmem((depth, width), kind) for kind in (BF, BF, F32)],
                *[dma((half, pieces))] * 8, *[dma((half, 2))] * 4, dma((2,)), dma((2,)),
                dma((half, 5)), dma((half, 5)), dma((2,)), dma((2,)),
                dma((half,)), dma((half,)), dma((2,)),
                dma((QUADS + 1,)), dma((QUADS + 1,)), pltpu.SemaphoreType.REGULAR,
            ],
            compiler_params=pltpu.CompilerParams(
                collective_id=0, has_side_effects=True, vmem_limit_bytes=40 << 20),
        )(*[pltpu.with_memory_space_constraint(x, pltpu.HBM) for x in (
            hidden, stash, skip_store, cotan, entry, loss_grad, wqkv, wout, region)])
        return pl.pallas_call(
            flush,
            out_shape=tuple(jax.ShapeDtypeStruct(x.shape, x.dtype) for x in outs),
            in_specs=[pl.BlockSpec(memory_space=pltpu.VMEM)] * 4,
            out_specs=[pl.BlockSpec(memory_space=pltpu.HBM)] * 4,
            scratch_shapes=[dma((4,))],
            compiler_params=pltpu.CompilerParams(vmem_limit_bytes=16 << 20),
        )(*outs)

    return jax.shard_map(
        step, mesh=mesh, in_specs=in_specs, out_specs=out_specs, check_vma=False
    )
```

```python
import functools

import jax
import jax.numpy as jnp
from jax import lax
from jax.experimental import pallas as pl
from jax.experimental.pallas import tpu as pltpu
from jax.sharding import PartitionSpec as P

HEADS = 8
HEAD_DIM = 64
WINDOW = 144
QUAD = 4 * HEAD_DIM
QUADS = HEADS // 4
BF = jnp.bfloat16
F32 = jnp.float32
MESH = pl.DeviceIdType.MESH


def mm(a, b, ca=1, cb=0):
    return lax.dot_general(a, b, (((ca,), (cb,)), ((), ())), preferred_element_type=F32)


def stats(u):
    up = u.astype(F32)
    centred = up - jnp.mean(up, axis=-1, keepdims=True)
    scale = lax.rsqrt(jnp.mean(centred * centred, axis=-1, keepdims=True) + 1e-05)
    return centred * scale, scale


def flush(*refs):
    srcs, dsts, sems = refs[0:4], refs[4:8], refs[8]
    stores = []
    for i in range(4):
        rows = srcs[i].shape[1]
        step = max(16, rows // 4 // 16 * 16) if i >= 2 else rows
        for at in range(0, rows, step):
            part = pl.ds(at, min(step, rows - at))
            stores.append(pltpu.make_async_copy(
                srcs[i].at[0, part], dsts[i].at[0, part], sems.at[len(stores)]))
    for store in stores:
        store.start()
    for store in stores:
        store.wait()


def kernel(n, segs, hid_in, stash_in, skip, cot_in, ent_in, lgrad_in, wq, wo, reg_in,
           acts, grads, gq, go,
           hid, stash, ent, gall, regs, lsem,
           wqf, wof, skin, yin, ysend, dsend, joined, nrm, nrmf, proj, projf, nt, ct, dproj, ctx,
           prob, same4, norm32, scales,
           q1s, q1r, qkeep, o1s, o1r, okeep,
           xs, xr, ys, yr, cs, cr, es, er, wxs, wxr, wcs, wcr, ms, mr, vs, vr,
           ksend, krecv, dss, dsr, ysem, p1s, p1r, ready):
    rows, width = hid_in.shape[1], hid_in.shape[2]
    half = n // 2
    depth = wq.shape[1]
    me = lax.axis_index("dp")
    seg = lax.axis_index("segment")
    grp = lax.axis_index("groups")
    chip, core = me // 2, me % 2
    other = 1 - core
    mate = chip * 2 + other
    mirror = segs - 1 - seg
    encoder = seg < segs // 2
    decoder = seg >= segs // 2
    last = seg == segs - 1

    def peer(off):
        return lax.rem(chip + off, half)

    loads = [pltpu.make_async_copy(src, dst, lsem.at[i]) for i, (src, dst) in enumerate((
        (stash_in.at[0], stash.at[0]), (cot_in.at[0], gall.at[0, 0]), (reg_in, regs[0]),
        (wq.at[0], wqf.at[me]), (wo.at[0], wof.at[me]), (hid_in.at[0], hid), (ent_in.at[0], ent)))]
    for load in loads:
        load.start()
    own_loss = pltpu.make_async_copy(lgrad_in.at[0], gall.at[0, 1], lsem.at[len(loads)])

    @pl.when(last)
    def _():
        own_loss.start()

    barrier = pltpu.get_barrier_semaphore()

    def greet(**where):
        pl.semaphore_signal(barrier, inc=1, device_id=where, device_id_type=MESH)

    greet(groups=1 - grp)
    for off in range(1, half):
        greet(dp=peer(off) * 2 + core)

    @pl.when(seg > 0)
    def _():
        greet(segment=seg - 1)

    @pl.when(seg < segs - 1)
    def _():
        greet(segment=seg + 1)

    greet(dp=mate)
    count = half + 1 + jnp.where(seg > 0, 1, 0)
    pl.semaphore_wait(barrier, count + jnp.where(seg < segs - 1, 1, 0))

    def remote(src, dst, ssem, rsem, **where):
        return pltpu.make_async_remote_copy(
            src_ref=src, dst_ref=dst, send_sem=ssem, recv_sem=rsem,
            device_id=where, device_id_type=MESH)

    sent = []

    def send(copy):
        copy.start()
        sent.append(copy)

    span = depth // 2
    size = 16
    pieces = range(span // size)
    parts = range(2)
    wspan = depth // 2

    def wq_rows(ref, lead, k, group):
        return ref.at[lead, pl.ds(pl.multiple_of(group * span + k * size, size), size)]

    def wo_rows(ref, lead, k):
        return ref.at[lead, pl.ds(k * wspan, wspan)]

    for k in pieces:
        for off in range(1, half):
            send(remote(wq_rows(wq, 0, k, grp), wq_rows(wqf, me, k, grp),
                        xs.at[off, k], xr.at[chip, k], dp=peer(off) * 2 + core))
    for k in parts:
        for off in range(1, half):
            send(remote(wo_rows(wo, 0, k), wo_rows(wof, me, k),
                        wxs.at[off, k], wxr.at[chip, k], dp=peer(off) * 2 + core))
    send(remote(wq.at[0], wqf.at[me], ms.at[0], mr.at[0], dp=mate))
    send(remote(wo.at[0], wof.at[me], ms.at[1], mr.at[1], dp=mate))

    def pass_on(k, off, group, ssem, rsem, **where):
        block = wq_rows(wqf, peer(off) * 2 + core, k, group)
        return remote(block, block, ssem.at[peer(off), k], rsem.at[peer(off), k], **where)

    def from_x(k):
        for off in range(1, half):
            pass_on(k, off, grp, xs, xr, dp=mate).wait_recv()
            send(pass_on(k, off, grp, ys, yr, groups=1 - grp))
            send(pass_on(k, off, grp, cs, cr, dp=mate))

    def from_y(k):
        for off in range(1, half):
            pass_on(k, off, 1 - grp, ys, yr, groups=1 - grp).wait_recv()
            send(pass_on(k, off, 1 - grp, es, er, dp=mate))

    def wo_from_x(k):
        for off in range(1, half):
            block = wo_rows(wof, peer(off) * 2 + core, k)
            remote(block, block, wxs.at[off, k], wxr.at[peer(off), k], dp=mate).wait_recv()
            send(remote(block, block, wcs.at[peer(off), k], wcr.at[peer(off), k], dp=mate))

    def from_core():
        for k in pieces:
            for off in range(1, half):
                for group, rsem in ((grp, cr), (1 - grp, er)):
                    block = wq_rows(wqf, peer(off) * 2 + other, k, group)
                    remote(block, block, cs.at[peer(off), k], rsem.at[peer(off), k],
                           dp=mate).wait_recv()

    def wo_from_core():
        for k in parts:
            for off in range(1, half):
                block = wo_rows(wof, peer(off) * 2 + other, k)
                remote(block, block, wcs.at[peer(off), k], wcr.at[peer(off), k],
                       dp=mate).wait_recv()

    def from_mate(w, ref):
        remote(ref.at[mate], ref.at[mate], ms.at[w], mr.at[w], dp=mate).wait_recv()

    def window_copies(off):
        return [remote(src, dst, vs.at[off, i], vr.at[off, i], dp=peer(off) * 2 + core)
                for i, (src, dst) in enumerate((
                    (stash_in.at[0, 0], stash.at[off, 0]), (cot_in.at[0], gall.at[off, 0]),
                    (reg_in, regs[off]), (stash_in.at[0, 1], stash.at[off, 1])))]

    def loss_copy(off):
        return remote(lgrad_in.at[0], gall.at[off, 1], vs.at[off, 4], vr.at[off, 4],
                      dp=peer(off) * 2 + core)

    def send_windows():
        for off in range(1, half):
            for copy in window_copies(off):
                send(copy)

            @pl.when(last)
            def _():
                loss_copy(off).start()

    def skip_copy(t):
        return remote(skip.at[0, t], skin.at[t], ksend.at[t], krecv.at[t], segment=mirror)

    def announce():
        pl.semaphore_signal(ready, inc=1, device_id={"segment": seg - 1}, device_id_type=MESH)

    def chain(here):
        @pl.when(here)
        def _():
            pl.semaphore_wait(ready, 1)

        @pl.when(jnp.logical_and(here, seg > 0))
        def _():
            announce()

    near = seg == segs // 2 - 1

    @pl.when(near)
    def _():
        skip_copy(0).start()

    if segs > 2:
        @pl.when(seg == segs - 2)
        def _():
            announce()

    for load in loads[:3]:
        load.wait()

    scale = HEAD_DIM ** (-0.5)
    lane = lax.broadcasted_iota(jnp.int32, (rows, QUAD), 1)
    heads = [jnp.logical_and(lane >= h * HEAD_DIM, lane < (h + 1) * HEAD_DIM).astype(F32)
             for h in range(4)]
    ones = [h.astype(BF) for h in heads]
    eighths = [(h * scale).astype(BF) for h in heads]
    left = lax.broadcasted_iota(jnp.int32, (rows, QUAD // 2), 1) < HEAD_DIM

    def masks(j):
        labels = jnp.broadcast_to(regs[j][...], (16, rows))
        onehot = (lax.broadcasted_iota(jnp.int32, (16, rows), 0) == labels).astype(F32)
        wide = jnp.concatenate([onehot] * 4, axis=1).astype(BF)
        same4[j] = mm(onehot.astype(BF), wide, 0, 0)

    def at(t, j):
        return (j * 2 + t) * rows

    def stack(x, by):
        return jnp.concatenate([x * h for h in by], axis=0)

    def fold(x):
        return jnp.concatenate(
            [jnp.where(left, x[2 * i * rows:(2 * i + 1) * rows, i * QUAD // 2:(i + 1) * QUAD // 2],
                       x[(2 * i + 1) * rows:(2 * i + 2) * rows, i * QUAD // 2:(i + 1) * QUAD // 2])
             for i in range(2)], axis=1)

    def part(ref, r, p, which):
        return ref[r:r + rows, which * width + p * QUAD:which * width + (p + 1) * QUAD]

    def softmax(ref, r, p, j):
        scores = mm(part(ref, r, p, 1), stack(part(ref, r, p, 0), eighths), 1, 1)
        scores = jnp.where(same4[j] > 0.5, scores, F32(-1000000000.0))
        e = jnp.exp(scores - jnp.max(scores, axis=0, keepdims=True))
        return e * (1.0 / jnp.sum(e, axis=0, keepdims=True))

    masks(0)
    for t in range(2):
        normal, inverse = stats(stash[0, t])
        norm32[t] = normal
        scales[t] = jnp.broadcast_to(inverse, (rows, 128))
        nrm[at(t, 0):at(t, 0) + rows] = normal.astype(BF)

    chain(seg == segs - 3)
    from_x(0)
    chain(seg < segs - 3)

    @pl.when(jnp.logical_and(encoder, seg < segs // 2 - 1))
    def _():
        skip_copy(0).start()

    for k in pieces[1:]:
        from_x(k)
    send_windows()
    for load in loads[3:]:
        load.wait()
    middle = len(pieces) // 2
    for k in pieces[:middle]:
        from_y(k)
    wo_from_x(0)
    for k in pieces[middle:-1]:
        from_y(k)
    wo_from_x(1)
    for k in pieces[-1:]:
        from_y(k)

    @pl.when(encoder)
    def _():
        skip_copy(1).start()

    from_mate(0, wqf)
    from_core()

    def w_qkv():
        return wqf[...].reshape(width, 3 * width)

    def w_out():
        return wof[...].reshape(width, width)

    def project(t, j):
        r = at(t, j)
        proj[r:r + rows] = mm(nrm[r:r + rows], w_qkv()).astype(BF)

    project(0, 0)

    def quad_backward(t, j, p, weights_f32, dctx):
        r = at(t, j)
        d4 = stack(dctx[:, p * QUAD:(p + 1) * QUAD], ones)
        d_attn = mm(part(proj, r, p, 2), d4, 1, 1)
        d_scores = (weights_f32 * (
            d_attn - jnp.sum(d_attn * weights_f32, axis=0, keepdims=True))).astype(BF)
        dq = fold(mm(d_scores, part(proj, r, p, 1), 0, 0)) * scale
        dk = mm(d_scores, stack(part(proj, r, p, 0), eighths))
        dv = mm(weights_f32.astype(BF), d4)
        for i, x in enumerate((dq, dk, dv)):
            dproj[r:r + rows, i * width + p * QUAD:i * width + (p + 1) * QUAD] = x.astype(BF)

    def context_of(ref, r, p, weights_f32):
        return fold(mm(weights_f32.astype(BF), part(ref, r, p, 2), 0, 0)).astype(BF)

    def input_cotangent(t):
        r = at(t, 0)
        d_norm = mm(dproj[r:r + rows], w_qkv(), 1, 1).astype(BF).astype(F32)
        normal, inverse = norm32[t], scales[t][:, 0:1]
        mean = jnp.mean(d_norm, axis=-1, keepdims=True)
        along = jnp.mean(d_norm * normal, axis=-1, keepdims=True)
        return (gall[0, t].astype(F32) + inverse * (d_norm - mean - normal * along)).astype(BF)

    def forward(u):
        nrmf[...] = stats(u)[0].astype(BF)
        projf[...] = mm(nrmf[...], w_qkv()).astype(BF)
        outs = [context_of(projf, 0, p, softmax(projf, 0, p, 0)) for p in range(QUADS)]
        return (u.astype(F32) + mm(jnp.concatenate(outs, axis=1), w_out())).astype(BF)

    def d_ctx(t, j):
        return mm(gall[j, t], w_out(), 1, 1).astype(BF)

    quad = chip * 2 * depth // QUAD

    def attend(t, j):
        for p in range(QUADS):
            prob[t, j, p] = softmax(proj, at(t, j), p, j)

    def keep_context(t, j):
        r = at(t, j)
        values = proj[r:r + rows, pl.ds(pl.multiple_of(2 * width + quad * QUAD, QUAD), QUAD)]
        weights = prob[t, j, quad].astype(BF)
        ctx[r:r + rows] = fold(mm(weights, values, 0, 0)).astype(BF)

    def backward(t, j, dctx):
        for p in range(QUADS):
            quad_backward(t, j, p, prob[t, j, p], dctx)

    attend(0, 0)
    from_mate(1, wof)
    wo_from_core()
    dctx = d_ctx(0, 0)
    backward(0, 0, dctx)
    dsend[...] = input_cotangent(0)

    def d_copy(off):
        return remote(dsend, gall.at[off, 1], dss.at[off], dsr.at[off],
                      segment=seg - 1, dp=peer(off) * 2 + core)

    @pl.when(seg > 0)
    def _():
        for off in range(half):
            d_copy(off).start()

    @pl.when(decoder)
    def _():
        skip_copy(0).wait_recv()
        joined[...] = (hid[...].astype(F32) + skin[0].astype(F32)).astype(BF)

    @pl.when(encoder)
    def _():
        joined[...] = hid[...]

    ysend[...] = forward(joined[...])

    def y_copy():
        return remote(ysend, yin, ysem.at[0], ysem.at[1], segment=seg + 1)

    @pl.when(seg < segs - 1)
    def _():
        y_copy().start()

    project(1, 0)
    attend(1, 0)

    def peer_window(t, j, copies):
        for copy in copies:
            copy.wait_recv()
        if t == 0:
            masks(j)
        r = at(t, j)
        nrm[r:r + rows] = stats(stash[j, t])[0].astype(BF)
        project(t, j)

    for j in range(1, half):
        peer_window(0, j, window_copies(j)[:3])
        attend(0, j)
        backward(0, j, d_ctx(0, j))
    for j in range(1, half):
        peer_window(1, j, window_copies(j)[3:])
        attend(1, j)
    for j in range(half):
        for t in range(2):
            keep_context(t, j)

    def columns_of(ref, first):
        if ref.shape[1] == 2 * depth:
            return ref[...]
        return ref[:, pl.ds(pl.multiple_of(first, 2 * depth), 2 * depth)]

    nt[...] = columns_of(nrm, chip * 2 * depth).T
    ct[...] = columns_of(ctx, chip * 2 * depth - quad * QUAD).T

    def cotangent_arrives(j):
        @pl.when(seg < segs - 1)
        def _():
            d_copy(j).wait_recv()

        @pl.when(last)
        def _():
            if j == 0:
                own_loss.wait()
            else:
                loss_copy(j).wait_recv()

    terms = [(o1s, o1r, okeep, 0)] + [
        (q1s.at[p], q1r.at[p], qkeep.at[p], 1 + p) for p in range(QUADS)]

    def hop(term):
        s1, r1, _, i = term
        return remote(s1, r1, p1s.at[i], p1r.at[i], dp=mate)

    def open_term(term, left, right):
        s1, _, keep, _ = term
        keep[...] = mm(left[...], right).reshape(keep.shape)
        s1[...] = keep[other].astype(BF)
        hop(term).start()

    cotangent_arrives(0)
    dctx = d_ctx(1, 0)
    for p in range(QUADS):
        quad_backward(1, 0, p, prob[1, 0, p], dctx)
    grads[0] = input_cotangent(1)
    for j in range(1, half):
        cotangent_arrives(j)
    open_term(terms[0], ct, gall[...].reshape(2 * half * rows, width))
    dctxs = [d_ctx(1, j) for j in range(1, half)]
    for p in range(QUADS):
        for j in range(1, half):
            quad_backward(1, j, p, prob[1, j, p], dctxs[j - 1])
        cols = [dproj[:, i * width + p * QUAD:i * width + (p + 1) * QUAD] for i in range(3)]
        open_term(terms[1 + p], nt, jnp.concatenate(cols, axis=1))

    @pl.when(seg == 0)
    def _():
        joined[...] = ent[...]

    @pl.when(seg > 0)
    def _():
        y_copy().wait_recv()

    @pl.when(jnp.logical_and(seg > 0, encoder))
    def _():
        joined[...] = yin[...]

    @pl.when(decoder)
    def _():
        skip_copy(1).wait_recv()
        joined[...] = (yin[...].astype(F32) + skin[1].astype(F32)).astype(BF)

    acts[0] = forward(joined[...])

    def close_term(term):
        hop(term).wait_recv()
        return term[2][core] + term[1][...].astype(F32)

    go[0] = close_term(terms[0])
    for p in range(QUADS):
        total = close_term(terms[1 + p])
        for i in range(3):
            gq[0, :, i * width + p * QUAD:i * width + (p + 1) * QUAD] = (
                total[:, i * QUAD:(i + 1) * QUAD])

    for copy in sent:
        copy.wait_send()
    for term in terms:
        hop(term).wait_send()

    @pl.when(last)
    def _():
        for off in range(1, half):
            loss_copy(off).wait_send()

    @pl.when(encoder)
    def _():
        for t in range(2):
            skip_copy(t).wait_send()

    @pl.when(seg > 0)
    def _():
        for off in range(half):
            d_copy(off).wait_send()

    @pl.when(seg < segs - 1)
    def _():
        y_copy().wait_send()


def solution(mesh):
    n, segs = mesh.shape["dp"], mesh.shape["segment"]
    half = n // 2
    in_specs = (
        P("segment", ("groups", "dp"), None),
        P("segment", None, ("groups", "dp"), None),
        P("segment", None, ("groups", "dp"), None),
        P("segment", ("groups", "dp"), None),
        P(None, ("groups", "dp"), None),
        P(None, ("groups", "dp"), None),
        P("segment", "dp", None),
        P("segment", "dp", None),
        P("segment", ("groups", "dp")),
    )
    out_specs = (
        P("segment", ("groups", "dp"), None),
        P("segment", ("groups", "dp"), None),
        P(("groups", "segment"), "dp", None),
        P(("groups", "segment"), "dp", None),
    )

    def step(hidden, stash, skip_store, cotan, entry, loss_grad, wqkv, wout, region):
        rows, width = hidden.shape[1:]
        depth = wqkv.shape[1]
        pieces = depth // 32
        vmem, dma = pltpu.VMEM, pltpu.SemaphoreType.DMA
        block = vmem((rows, width), BF)
        windows = 2 * half * rows

        outs = pl.pallas_call(
            functools.partial(kernel, n, segs),
            out_shape=(
                vmem(hidden.shape, BF), vmem(hidden.shape, BF),
                vmem(wqkv.shape, F32), vmem(wout.shape, F32),
            ),
            in_specs=[pl.BlockSpec(memory_space=pltpu.HBM)] * 9,
            out_specs=[pl.BlockSpec(memory_space=pltpu.VMEM)] * 4,
            scratch_shapes=[
                block, vmem((half, 2, rows, width), BF), block, vmem((half, 2, rows, width), BF),
                [vmem(region.shape, region.dtype) for _ in range(half)], dma((8,)),
                vmem((n, depth, 3 * width), BF), vmem((n, depth, width), BF),
                vmem((2, rows, width), BF), block, block, block, block,
                vmem((windows, width), BF), block,
                vmem((windows, 3 * width), BF), vmem((rows, 3 * width), BF),
                vmem((2 * depth, windows), BF), vmem((2 * depth, windows), BF),
                vmem((windows, 3 * width), BF), vmem((windows, QUAD), BF),
                vmem((2, half, QUADS, rows, 4 * rows), F32), vmem((half, rows, 4 * rows), F32),
                vmem((2, rows, width), F32), vmem((2, rows, 128), F32),
                *[vmem((QUADS, depth, 3 * QUAD), BF)] * 2, vmem((QUADS, 2, depth, 3 * QUAD), F32),
                *[vmem((depth, width), BF)] * 2, vmem((2, depth, width), F32),
                *[dma((half, pieces))] * 8, *[dma((half, 2))] * 4, dma((2,)), dma((2,)),
                dma((half, 5)), dma((half, 5)), dma((2,)), dma((2,)),
                dma((half,)), dma((half,)), dma((2,)),
                dma((QUADS + 1,)), dma((QUADS + 1,)), pltpu.SemaphoreType.REGULAR,
            ],
            compiler_params=pltpu.CompilerParams(
                collective_id=0, has_side_effects=True, vmem_limit_bytes=40 << 20),
        )(*[pltpu.with_memory_space_constraint(x, pltpu.HBM) for x in (
            hidden, stash, skip_store, cotan, entry, loss_grad, wqkv, wout, region)])
        return pl.pallas_call(
            flush,
            out_shape=tuple(jax.ShapeDtypeStruct(x.shape, x.dtype) for x in outs),
            in_specs=[pl.BlockSpec(memory_space=pltpu.VMEM)] * 4,
            out_specs=[pl.BlockSpec(memory_space=pltpu.HBM)] * 4,
            scratch_shapes=[dma((16,))],
            compiler_params=pltpu.CompilerParams(vmem_limit_bytes=16 << 20),
        )(*outs)

    return jax.shard_map(
        step, mesh=mesh, in_specs=in_specs, out_specs=out_specs, check_vma=False
    )
```

```python
import functools

import jax
import jax.numpy as jnp
from jax import lax
from jax.experimental import pallas as pl
from jax.experimental.pallas import tpu as pltpu
from jax.sharding import PartitionSpec as P

HEADS = 8
HEAD_DIM = 64
WINDOW = 144
QUAD = 4 * HEAD_DIM
QUADS = HEADS // 4
BF = jnp.bfloat16
F32 = jnp.float32
MESH = pl.DeviceIdType.MESH


def mm(a, b, ca=1, cb=0):
    return lax.dot_general(a, b, (((ca,), (cb,)), ((), ())), preferred_element_type=F32)


def stats(u):
    up = u.astype(F32)
    centred = up - jnp.mean(up, axis=-1, keepdims=True)
    scale = lax.rsqrt(jnp.mean(centred * centred, axis=-1, keepdims=True) + 1e-05)
    return centred * scale, scale


def flush(*refs):
    srcs, dsts, sems = refs[0:4], refs[4:8], refs[8]
    stores = []
    for i in range(4):
        rows = srcs[i].shape[1]
        step = max(16, rows // 4 // 16 * 16) if i >= 2 else rows
        for at in range(0, rows, step):
            part = pl.ds(at, min(step, rows - at))
            stores.append(pltpu.make_async_copy(
                srcs[i].at[0, part], dsts[i].at[0, part], sems.at[len(stores)]))
    for store in stores:
        store.start()
    for store in stores:
        store.wait()


def kernel(n, segs, hid_in, stash_in, skip, cot_in, ent_in, lgrad_in, wq, wo, reg_in,
           acts, grads, gq, go,
           hid, stash, ent, gall, regs, lsem,
           wqf, wof, skin, yin, ysend, dsend, joined, nrm, nrmf, proj, projf, nt, ct, dproj, ctx,
           prob, same4, norm32, scales,
           q1s, q1r, qkeep, o1s, o1r, okeep,
           xs, xr, ys, yr, cs, cr, es, er, wxs, wxr, wcs, wcr, ms, mr, vs, vr,
           ksend, krecv, dss, dsr, ysem, p1s, p1r, ready):
    rows, width = hid_in.shape[1], hid_in.shape[2]
    half = n // 2
    depth = wq.shape[1]
    me = lax.axis_index("dp")
    seg = lax.axis_index("segment")
    grp = lax.axis_index("groups")
    chip, core = me // 2, me % 2
    other = 1 - core
    mate = chip * 2 + other
    mirror = segs - 1 - seg
    encoder = seg < segs // 2
    decoder = seg >= segs // 2
    last = seg == segs - 1

    def peer(off):
        return lax.rem(chip + off, half)

    loads = [pltpu.make_async_copy(src, dst, lsem.at[i]) for i, (src, dst) in enumerate((
        (stash_in.at[0], stash.at[0]), (cot_in.at[0], gall.at[0, 0]), (reg_in, regs[0]),
        (wq.at[0], wqf.at[me]), (wo.at[0], wof.at[me]), (hid_in.at[0], hid), (ent_in.at[0], ent)))]
    for load in loads:
        load.start()
    own_loss = pltpu.make_async_copy(lgrad_in.at[0], gall.at[1, 0], lsem.at[len(loads)])

    @pl.when(last)
    def _():
        own_loss.start()

    barrier = pltpu.get_barrier_semaphore()

    def greet(**where):
        pl.semaphore_signal(barrier, inc=1, device_id=where, device_id_type=MESH)

    greet(groups=1 - grp)
    for off in range(1, half):
        greet(dp=peer(off) * 2 + core)

    @pl.when(seg > 0)
    def _():
        greet(segment=seg - 1)

    @pl.when(seg < segs - 1)
    def _():
        greet(segment=seg + 1)

    greet(dp=mate)
    count = half + 1 + jnp.where(seg > 0, 1, 0)
    pl.semaphore_wait(barrier, count + jnp.where(seg < segs - 1, 1, 0))

    def remote(src, dst, ssem, rsem, **where):
        return pltpu.make_async_remote_copy(
            src_ref=src, dst_ref=dst, send_sem=ssem, recv_sem=rsem,
            device_id=where, device_id_type=MESH)

    sent = []

    def send(copy):
        copy.start()
        sent.append(copy)

    span = depth // 2
    size = 16
    pieces = range(span // size)
    parts = range(2)
    wspan = depth // 2

    def wq_rows(ref, lead, k, group):
        return ref.at[lead, pl.ds(pl.multiple_of(group * span + k * size, size), size)]

    def wo_rows(ref, lead, k):
        return ref.at[lead, pl.ds(k * wspan, wspan)]

    for k in pieces:
        for off in range(1, half):
            send(remote(wq_rows(wq, 0, k, grp), wq_rows(wqf, me, k, grp),
                        xs.at[off, k], xr.at[chip, k], dp=peer(off) * 2 + core))
    for k in parts:
        for off in range(1, half):
            send(remote(wo_rows(wo, 0, k), wo_rows(wof, me, k),
                        wxs.at[off, k], wxr.at[chip, k], dp=peer(off) * 2 + core))
    send(remote(wq.at[0], wqf.at[me], ms.at[0], mr.at[0], dp=mate))
    send(remote(wo.at[0], wof.at[me], ms.at[1], mr.at[1], dp=mate))

    def pass_on(k, off, group, ssem, rsem, **where):
        block = wq_rows(wqf, peer(off) * 2 + core, k, group)
        return remote(block, block, ssem.at[peer(off), k], rsem.at[peer(off), k], **where)

    def from_x(k):
        for off in range(1, half):
            pass_on(k, off, grp, xs, xr, dp=mate).wait_recv()
            send(pass_on(k, off, grp, ys, yr, groups=1 - grp))
            send(pass_on(k, off, grp, cs, cr, dp=mate))

    def from_y(k):
        for off in range(1, half):
            pass_on(k, off, 1 - grp, ys, yr, groups=1 - grp).wait_recv()
            send(pass_on(k, off, 1 - grp, es, er, dp=mate))

    def wo_from_x(k):
        for off in range(1, half):
            block = wo_rows(wof, peer(off) * 2 + core, k)
            remote(block, block, wxs.at[off, k], wxr.at[peer(off), k], dp=mate).wait_recv()
            send(remote(block, block, wcs.at[peer(off), k], wcr.at[peer(off), k], dp=mate))

    def from_core():
        for k in pieces:
            for off in range(1, half):
                for group, rsem in ((grp, cr), (1 - grp, er)):
                    block = wq_rows(wqf, peer(off) * 2 + other, k, group)
                    remote(block, block, cs.at[peer(off), k], rsem.at[peer(off), k],
                           dp=mate).wait_recv()

    def wo_from_core():
        for k in parts:
            for off in range(1, half):
                block = wo_rows(wof, peer(off) * 2 + other, k)
                remote(block, block, wcs.at[peer(off), k], wcr.at[peer(off), k],
                       dp=mate).wait_recv()

    def from_mate(w, ref):
        remote(ref.at[mate], ref.at[mate], ms.at[w], mr.at[w], dp=mate).wait_recv()

    def window_copies(off):
        return [remote(src, dst, vs.at[off, i], vr.at[off, i], dp=peer(off) * 2 + core)
                for i, (src, dst) in enumerate((
                    (stash_in.at[0, 0], stash.at[off, 0]), (cot_in.at[0], gall.at[0, off]),
                    (reg_in, regs[off]), (stash_in.at[0, 1], stash.at[off, 1])))]

    def loss_copy(off):
        return remote(lgrad_in.at[0], gall.at[1, off], vs.at[off, 4], vr.at[off, 4],
                      dp=peer(off) * 2 + core)

    def send_windows():
        for off in range(1, half):
            for copy in window_copies(off):
                send(copy)

            @pl.when(last)
            def _():
                loss_copy(off).start()

    def skip_copy(t):
        return remote(skip.at[0, t], skin.at[t], ksend.at[t], krecv.at[t], segment=mirror)

    def announce():
        pl.semaphore_signal(ready, inc=1, device_id={"segment": seg - 1}, device_id_type=MESH)

    def chain(here):
        @pl.when(here)
        def _():
            pl.semaphore_wait(ready, 1)

        @pl.when(jnp.logical_and(here, seg > 0))
        def _():
            announce()

    near = seg == segs // 2 - 1

    @pl.when(near)
    def _():
        skip_copy(0).start()

    if segs > 2:
        @pl.when(seg == segs - 2)
        def _():
            announce()

    for load in loads[:3]:
        load.wait()

    scale = HEAD_DIM ** (-0.5)
    lane = lax.broadcasted_iota(jnp.int32, (rows, QUAD), 1)
    heads = [jnp.logical_and(lane >= h * HEAD_DIM, lane < (h + 1) * HEAD_DIM).astype(F32)
             for h in range(4)]
    ones = [h.astype(BF) for h in heads]
    eighths = [(h * scale).astype(BF) for h in heads]
    left = lax.broadcasted_iota(jnp.int32, (rows, QUAD // 2), 1) < HEAD_DIM

    def masks(j):
        labels = jnp.broadcast_to(regs[j][...], (16, rows))
        onehot = (lax.broadcasted_iota(jnp.int32, (16, rows), 0) == labels).astype(F32)
        wide = jnp.concatenate([onehot] * 4, axis=1).astype(BF)
        same4[j] = mm(onehot.astype(BF), wide, 0, 0)

    def at(t, j):
        return (t * half + j) * rows

    def stack(x, by):
        return jnp.concatenate([x * h for h in by], axis=0)

    def fold(x):
        return jnp.concatenate(
            [jnp.where(left, x[2 * i * rows:(2 * i + 1) * rows, i * QUAD // 2:(i + 1) * QUAD // 2],
                       x[(2 * i + 1) * rows:(2 * i + 2) * rows, i * QUAD // 2:(i + 1) * QUAD // 2])
             for i in range(2)], axis=1)

    def part(ref, r, p, which):
        return ref[r:r + rows, which * width + p * QUAD:which * width + (p + 1) * QUAD]

    def softmax(ref, r, p, j):
        scores = mm(part(ref, r, p, 1), stack(part(ref, r, p, 0), eighths), 1, 1)
        scores = jnp.where(same4[j] > 0.5, scores, F32(-1000000000.0))
        e = jnp.exp(scores - jnp.max(scores, axis=0, keepdims=True))
        return e * (1.0 / jnp.sum(e, axis=0, keepdims=True))

    masks(0)
    for t in range(2):
        normal, inverse = stats(stash[0, t])
        norm32[t] = normal
        scales[t] = jnp.broadcast_to(inverse, (rows, 128))
        nrm[at(t, 0):at(t, 0) + rows] = normal.astype(BF)

    chain(seg == segs - 3)
    from_x(0)
    chain(seg < segs - 3)

    @pl.when(jnp.logical_and(encoder, seg < segs // 2 - 1))
    def _():
        skip_copy(0).start()

    for k in pieces[1:]:
        from_x(k)
    send_windows()
    for load in loads[3:]:
        load.wait()
    middle = len(pieces) // 2
    for k in pieces[:middle]:
        from_y(k)
    wo_from_x(0)
    for k in pieces[middle:-1]:
        from_y(k)
    wo_from_x(1)
    for k in pieces[-1:]:
        from_y(k)

    @pl.when(encoder)
    def _():
        skip_copy(1).start()

    from_mate(0, wqf)
    from_core()

    def w_qkv():
        return wqf[...].reshape(width, 3 * width)

    def w_out():
        return wof[...].reshape(width, width)

    def project(t, j):
        r = at(t, j)
        proj[r:r + rows] = mm(nrm[r:r + rows], w_qkv()).astype(BF)

    project(0, 0)

    def quad_backward(t, j, p, weights_f32, dctx):
        r = at(t, j)
        d4 = stack(dctx[:, p * QUAD:(p + 1) * QUAD], ones)
        d_attn = mm(part(proj, r, p, 2), d4, 1, 1)
        d_scores = (weights_f32 * (
            d_attn - jnp.sum(d_attn * weights_f32, axis=0, keepdims=True))).astype(BF)
        dq = fold(mm(d_scores, part(proj, r, p, 1), 0, 0)) * scale
        dk = mm(d_scores, stack(part(proj, r, p, 0), eighths))
        dv = mm(weights_f32.astype(BF), d4)
        for i, x in enumerate((dq, dk, dv)):
            dproj[r:r + rows, i * width + p * QUAD:i * width + (p + 1) * QUAD] = x.astype(BF)

    def context_of(ref, r, p, weights_f32):
        return fold(mm(weights_f32.astype(BF), part(ref, r, p, 2), 0, 0)).astype(BF)

    def input_cotangent(t):
        r = at(t, 0)
        d_norm = mm(dproj[r:r + rows], w_qkv(), 1, 1).astype(BF).astype(F32)
        normal, inverse = norm32[t], scales[t][:, 0:1]
        mean = jnp.mean(d_norm, axis=-1, keepdims=True)
        along = jnp.mean(d_norm * normal, axis=-1, keepdims=True)
        return (gall[t, 0].astype(F32) + inverse * (d_norm - mean - normal * along)).astype(BF)

    def forward(u):
        nrmf[...] = stats(u)[0].astype(BF)
        projf[...] = mm(nrmf[...], w_qkv()).astype(BF)
        outs = [context_of(projf, 0, p, softmax(projf, 0, p, 0)) for p in range(QUADS)]
        return (u.astype(F32) + mm(jnp.concatenate(outs, axis=1), w_out())).astype(BF)

    def d_ctx(t, j):
        return mm(gall[t, j], w_out(), 1, 1).astype(BF)

    quad = chip * 2 * depth // QUAD

    def attend(t, j):
        for p in range(QUADS):
            prob[t, j, p] = softmax(proj, at(t, j), p, j)

    def keep_context(t, j):
        r = at(t, j)
        values = proj[r:r + rows, pl.ds(pl.multiple_of(2 * width + quad * QUAD, QUAD), QUAD)]
        weights = prob[t, j, quad].astype(BF)
        ctx[r:r + rows] = fold(mm(weights, values, 0, 0)).astype(BF)

    def backward(t, j, dctx):
        for p in range(QUADS):
            quad_backward(t, j, p, prob[t, j, p], dctx)

    attend(0, 0)
    from_mate(1, wof)
    wo_from_core()
    dctx = d_ctx(0, 0)
    backward(0, 0, dctx)
    dsend[...] = input_cotangent(0)

    def d_copy(off):
        return remote(dsend, gall.at[1, off], dss.at[off], dsr.at[off],
                      segment=seg - 1, dp=peer(off) * 2 + core)

    @pl.when(seg > 0)
    def _():
        for off in range(half):
            d_copy(off).start()

    @pl.when(decoder)
    def _():
        skip_copy(0).wait_recv()
        joined[...] = (hid[...].astype(F32) + skin[0].astype(F32)).astype(BF)

    @pl.when(encoder)
    def _():
        joined[...] = hid[...]

    ysend[...] = forward(joined[...])

    def y_copy():
        return remote(ysend, yin, ysem.at[0], ysem.at[1], segment=seg + 1)

    @pl.when(seg < segs - 1)
    def _():
        y_copy().start()

    project(1, 0)
    attend(1, 0)

    def peer_window(t, j, copies):
        for copy in copies:
            copy.wait_recv()
        if t == 0:
            masks(j)
        r = at(t, j)
        nrm[r:r + rows] = stats(stash[j, t])[0].astype(BF)
        project(t, j)

    for j in range(1, half):
        peer_window(0, j, window_copies(j)[:3])
        attend(0, j)
        backward(0, j, d_ctx(0, j))
    for j in range(1, half):
        peer_window(1, j, window_copies(j)[3:])
        attend(1, j)
    for j in range(half):
        for t in range(2):
            keep_context(t, j)

    def columns_of(ref, first):
        if ref.shape[1] == 2 * depth:
            return ref[...]
        return ref[:, pl.ds(pl.multiple_of(first, 2 * depth), 2 * depth)]

    ready_rows = (half + 1) * rows
    for src, dest, first in ((nrm, nt, chip * 2 * depth), (ctx, ct, chip * 2 * depth - quad * QUAD)):
        block = columns_of(src, first)
        dest[0][...] = block[:ready_rows].T
        dest[1][...] = block[ready_rows:].T

    def cotangent_arrives(j):
        @pl.when(seg < segs - 1)
        def _():
            d_copy(j).wait_recv()

        @pl.when(last)
        def _():
            if j == 0:
                own_loss.wait()
            else:
                loss_copy(j).wait_recv()

    terms = [(o1s, o1r, okeep, 0)] + [
        (q1s.at[p], q1r.at[p], qkeep.at[p], 1 + p) for p in range(QUADS)]

    def hop(term):
        s1, r1, _, i = term
        return remote(s1, r1, p1s.at[i], p1r.at[i], dp=mate)

    def begin_term(term, left, right):
        keep = term[2]
        keep[...] = mm(left[0][...], right).reshape(keep.shape)

    def open_term(term, left, right):
        s1, _, keep, _ = term
        keep[...] = keep[...] + mm(left[1][...], right).reshape(keep.shape)
        s1[...] = keep[other].astype(BF)
        hop(term).start()

    cotangent_arrives(0)
    dctx = d_ctx(1, 0)
    for p in range(QUADS):
        quad_backward(1, 0, p, prob[1, 0, p], dctx)
    grads[0] = input_cotangent(1)

    def projection_rows(p, first, last):
        return jnp.concatenate(
            [dproj[first:last, i * width + p * QUAD:i * width + (p + 1) * QUAD]
             for i in range(3)], axis=1)

    begin_term(terms[0], ct, jnp.concatenate(
        [gall[0].reshape(half * rows, width), gall[1, 0]], axis=0))
    for p in range(QUADS):
        begin_term(terms[1 + p], nt, projection_rows(p, 0, ready_rows))
    for j in range(1, half):
        cotangent_arrives(j)
    open_term(terms[0], ct, gall[1, 1:].reshape((half - 1) * rows, width))
    dctxs = [d_ctx(1, j) for j in range(1, half)]
    for p in range(QUADS):
        for j in range(1, half):
            quad_backward(1, j, p, prob[1, j, p], dctxs[j - 1])
        open_term(terms[1 + p], nt, projection_rows(p, ready_rows, 2 * half * rows))

    @pl.when(seg == 0)
    def _():
        joined[...] = ent[...]

    @pl.when(seg > 0)
    def _():
        y_copy().wait_recv()

    @pl.when(jnp.logical_and(seg > 0, encoder))
    def _():
        joined[...] = yin[...]

    @pl.when(decoder)
    def _():
        skip_copy(1).wait_recv()
        joined[...] = (yin[...].astype(F32) + skin[1].astype(F32)).astype(BF)

    acts[0] = forward(joined[...])

    def close_term(term):
        hop(term).wait_recv()
        return term[2][core] + term[1][...].astype(F32)

    go[0] = close_term(terms[0])
    for p in range(QUADS):
        total = close_term(terms[1 + p])
        for i in range(3):
            gq[0, :, i * width + p * QUAD:i * width + (p + 1) * QUAD] = (
                total[:, i * QUAD:(i + 1) * QUAD])

    for copy in sent:
        copy.wait_send()
    for term in terms:
        hop(term).wait_send()

    @pl.when(last)
    def _():
        for off in range(1, half):
            loss_copy(off).wait_send()

    @pl.when(encoder)
    def _():
        for t in range(2):
            skip_copy(t).wait_send()

    @pl.when(seg > 0)
    def _():
        for off in range(half):
            d_copy(off).wait_send()

    @pl.when(seg < segs - 1)
    def _():
        y_copy().wait_send()


def solution(mesh):
    n, segs = mesh.shape["dp"], mesh.shape["segment"]
    half = n // 2
    in_specs = (
        P("segment", ("groups", "dp"), None),
        P("segment", None, ("groups", "dp"), None),
        P("segment", None, ("groups", "dp"), None),
        P("segment", ("groups", "dp"), None),
        P(None, ("groups", "dp"), None),
        P(None, ("groups", "dp"), None),
        P("segment", "dp", None),
        P("segment", "dp", None),
        P("segment", ("groups", "dp")),
    )
    out_specs = (
        P("segment", ("groups", "dp"), None),
        P("segment", ("groups", "dp"), None),
        P(("groups", "segment"), "dp", None),
        P(("groups", "segment"), "dp", None),
    )

    def step(hidden, stash, skip_store, cotan, entry, loss_grad, wqkv, wout, region):
        rows, width = hidden.shape[1:]
        depth = wqkv.shape[1]
        pieces = depth // 32
        vmem, dma = pltpu.VMEM, pltpu.SemaphoreType.DMA
        block = vmem((rows, width), BF)
        windows = 2 * half * rows

        outs = pl.pallas_call(
            functools.partial(kernel, n, segs),
            out_shape=(
                vmem(hidden.shape, BF), vmem(hidden.shape, BF),
                vmem(wqkv.shape, F32), vmem(wout.shape, F32),
            ),
            in_specs=[pl.BlockSpec(memory_space=pltpu.HBM)] * 9,
            out_specs=[pl.BlockSpec(memory_space=pltpu.VMEM)] * 4,
            scratch_shapes=[
                block, vmem((half, 2, rows, width), BF), block, vmem((2, half, rows, width), BF),
                [vmem(region.shape, region.dtype) for _ in range(half)], dma((8,)),
                vmem((n, depth, 3 * width), BF), vmem((n, depth, width), BF),
                vmem((2, rows, width), BF), block, block, block, block,
                vmem((windows, width), BF), block,
                vmem((windows, 3 * width), BF), vmem((rows, 3 * width), BF),
                *[[vmem((2 * depth, (half + 1) * rows), BF), vmem((2 * depth, (half - 1) * rows), BF)]] * 2,
                vmem((windows, 3 * width), BF), vmem((windows, QUAD), BF),
                vmem((2, half, QUADS, rows, 4 * rows), F32), vmem((half, rows, 4 * rows), F32),
                vmem((2, rows, width), F32), vmem((2, rows, 128), F32),
                *[vmem((QUADS, depth, 3 * QUAD), BF)] * 2, vmem((QUADS, 2, depth, 3 * QUAD), F32),
                *[vmem((depth, width), BF)] * 2, vmem((2, depth, width), F32),
                *[dma((half, pieces))] * 8, *[dma((half, 2))] * 4, dma((2,)), dma((2,)),
                dma((half, 5)), dma((half, 5)), dma((2,)), dma((2,)),
                dma((half,)), dma((half,)), dma((2,)),
                dma((QUADS + 1,)), dma((QUADS + 1,)), pltpu.SemaphoreType.REGULAR,
            ],
            compiler_params=pltpu.CompilerParams(
                collective_id=0, has_side_effects=True, vmem_limit_bytes=40 << 20),
        )(*[pltpu.with_memory_space_constraint(x, pltpu.HBM) for x in (
            hidden, stash, skip_store, cotan, entry, loss_grad, wqkv, wout, region)])
        return pl.pallas_call(
            flush,
            out_shape=tuple(jax.ShapeDtypeStruct(x.shape, x.dtype) for x in outs),
            in_specs=[pl.BlockSpec(memory_space=pltpu.VMEM)] * 4,
            out_specs=[pl.BlockSpec(memory_space=pltpu.HBM)] * 4,
            scratch_shapes=[dma((16,))],
            compiler_params=pltpu.CompilerParams(vmem_limit_bytes=16 << 20),
        )(*outs)

    return jax.shard_map(
        step, mesh=mesh, in_specs=in_specs, out_specs=out_specs, check_vma=False
    )
```

```python
import functools

import jax
import jax.numpy as jnp
from jax import lax
from jax.experimental import pallas as pl
from jax.experimental.pallas import tpu as pltpu
from jax.sharding import PartitionSpec as P

HEADS = 8
HEAD_DIM = 64
WINDOW = 144
QUAD = 4 * HEAD_DIM
QUADS = HEADS // 4
BF = jnp.bfloat16
F32 = jnp.float32
MESH = pl.DeviceIdType.MESH


def mm(a, b, ca=1, cb=0):
    return lax.dot_general(a, b, (((ca,), (cb,)), ((), ())), preferred_element_type=F32)


def stats(u):
    up = u.astype(F32)
    centred = up - jnp.mean(up, axis=-1, keepdims=True)
    scale = lax.rsqrt(jnp.mean(centred * centred, axis=-1, keepdims=True) + 1e-05)
    return centred * scale, scale


def flush(*refs):
    srcs, dsts, sems = refs[0:4], refs[4:8], refs[8]
    stores = []
    for i in range(4):
        rows = srcs[i].shape[1]
        step = max(16, rows // 4 // 16 * 16) if i >= 2 else rows
        for at in range(0, rows, step):
            part = pl.ds(at, min(step, rows - at))
            stores.append(pltpu.make_async_copy(
                srcs[i].at[0, part], dsts[i].at[0, part], sems.at[len(stores)]))
    for store in stores:
        store.start()
    for store in stores:
        store.wait()


def kernel(n, segs, hid_in, stash_in, skip, cot_in, ent_in, lgrad_in, wq, wo, reg_in,
           acts, grads, gq, go,
           hid, stash, ent, gall, regs, lsem,
           wqf, wof, skin, yin, ysend, dsend, joined, nrm, nrmf, proj, projf, nt, ct, dproj, ctx,
           prob, same4, norm32, scales,
           q1s, q1r, qkeep, o1s, o1r, okeep,
           xs, xr, ys, yr, cs, cr, es, er, wxs, wxr, wcs, wcr, ms, mr, vs, vr,
           ksend, krecv, dss, dsr, ysem, p1s, p1r, ready):
    rows, width = hid_in.shape[1], hid_in.shape[2]
    half = n // 2
    depth = wq.shape[1]
    me = lax.axis_index("dp")
    seg = lax.axis_index("segment")
    grp = lax.axis_index("groups")
    chip, core = me // 2, me % 2
    other = 1 - core
    mate = chip * 2 + other
    mirror = segs - 1 - seg
    encoder = seg < segs // 2
    decoder = seg >= segs // 2
    last = seg == segs - 1

    def peer(off):
        return lax.rem(chip + off, half)

    loads = [pltpu.make_async_copy(src, dst, lsem.at[i]) for i, (src, dst) in enumerate((
        (stash_in.at[0], stash.at[0]), (cot_in.at[0], gall.at[0, 0]), (reg_in, regs[0]),
        (wq.at[0], wqf.at[me]), (wo.at[0], wof.at[me]), (hid_in.at[0], hid), (ent_in.at[0], ent)))]
    for load in loads:
        load.start()
    own_loss = pltpu.make_async_copy(lgrad_in.at[0], gall.at[1, 0], lsem.at[len(loads)])

    @pl.when(last)
    def _():
        own_loss.start()

    barrier = pltpu.get_barrier_semaphore()

    def greet(**where):
        pl.semaphore_signal(barrier, inc=1, device_id=where, device_id_type=MESH)

    greet(groups=1 - grp)
    for off in range(1, half):
        greet(dp=peer(off) * 2 + core)

    @pl.when(seg > 0)
    def _():
        greet(segment=seg - 1)

    @pl.when(seg < segs - 1)
    def _():
        greet(segment=seg + 1)

    greet(dp=mate)
    count = half + 1 + jnp.where(seg > 0, 1, 0)
    pl.semaphore_wait(barrier, count + jnp.where(seg < segs - 1, 1, 0))

    def remote(src, dst, ssem, rsem, **where):
        return pltpu.make_async_remote_copy(
            src_ref=src, dst_ref=dst, send_sem=ssem, recv_sem=rsem,
            device_id=where, device_id_type=MESH)

    sent = []

    def send(copy):
        copy.start()
        sent.append(copy)

    span = depth // 2
    size = 16
    pieces = range(span // size)
    parts = range(2)
    wspan = depth // 2

    def wq_rows(ref, lead, k, group):
        return ref.at[lead, pl.ds(pl.multiple_of(group * span + k * size, size), size)]

    def wo_rows(ref, lead, k):
        return ref.at[lead, pl.ds(k * wspan, wspan)]

    for k in pieces:
        for off in range(1, half):
            send(remote(wq_rows(wq, 0, k, grp), wq_rows(wqf, me, k, grp),
                        xs.at[off, k], xr.at[chip, k], dp=peer(off) * 2 + core))
    for k in parts:
        for off in range(1, half):
            send(remote(wo_rows(wo, 0, k), wo_rows(wof, me, k),
                        wxs.at[off, k], wxr.at[chip, k], dp=peer(off) * 2 + core))
    send(remote(wq.at[0], wqf.at[me], ms.at[0], mr.at[0], dp=mate))
    send(remote(wo.at[0], wof.at[me], ms.at[1], mr.at[1], dp=mate))

    def pass_on(k, off, group, ssem, rsem, **where):
        block = wq_rows(wqf, peer(off) * 2 + core, k, group)
        return remote(block, block, ssem.at[peer(off), k], rsem.at[peer(off), k], **where)

    def from_x(k):
        for off in range(1, half):
            pass_on(k, off, grp, xs, xr, dp=mate).wait_recv()
            send(pass_on(k, off, grp, ys, yr, groups=1 - grp))
            send(pass_on(k, off, grp, cs, cr, dp=mate))

    def from_y(k):
        for off in range(1, half):
            pass_on(k, off, 1 - grp, ys, yr, groups=1 - grp).wait_recv()
            send(pass_on(k, off, 1 - grp, es, er, dp=mate))

    def wo_from_x(k):
        for off in range(1, half):
            block = wo_rows(wof, peer(off) * 2 + core, k)
            remote(block, block, wxs.at[off, k], wxr.at[peer(off), k], dp=mate).wait_recv()
            send(remote(block, block, wcs.at[peer(off), k], wcr.at[peer(off), k], dp=mate))

    def from_core():
        for k in pieces:
            for off in range(1, half):
                for group, rsem in ((grp, cr), (1 - grp, er)):
                    block = wq_rows(wqf, peer(off) * 2 + other, k, group)
                    remote(block, block, cs.at[peer(off), k], rsem.at[peer(off), k],
                           dp=mate).wait_recv()

    def wo_from_core():
        for k in parts:
            for off in range(1, half):
                block = wo_rows(wof, peer(off) * 2 + other, k)
                remote(block, block, wcs.at[peer(off), k], wcr.at[peer(off), k],
                       dp=mate).wait_recv()

    def from_mate(w, ref):
        remote(ref.at[mate], ref.at[mate], ms.at[w], mr.at[w], dp=mate).wait_recv()

    def window_copies(off):
        return [remote(src, dst, vs.at[off, i], vr.at[off, i], dp=peer(off) * 2 + core)
                for i, (src, dst) in enumerate((
                    (stash_in.at[0, 0], stash.at[off, 0]), (cot_in.at[0], gall.at[0, off]),
                    (reg_in, regs[off]), (stash_in.at[0, 1], stash.at[off, 1])))]

    def loss_copy(off):
        return remote(lgrad_in.at[0], gall.at[1, off], vs.at[off, 4], vr.at[off, 4],
                      dp=peer(off) * 2 + core)

    def send_windows():
        for off in range(1, half):
            for copy in window_copies(off):
                send(copy)

            @pl.when(last)
            def _():
                loss_copy(off).start()

    def skip_copy(t):
        return remote(skip.at[0, t], skin.at[t], ksend.at[t], krecv.at[t], segment=mirror)

    def announce():
        pl.semaphore_signal(ready, inc=1, device_id={"segment": seg - 1}, device_id_type=MESH)

    def chain(here):
        @pl.when(here)
        def _():
            pl.semaphore_wait(ready, 1)

        @pl.when(jnp.logical_and(here, seg > 0))
        def _():
            announce()

    near = seg == segs // 2 - 1

    @pl.when(near)
    def _():
        skip_copy(0).start()

    if segs > 2:
        @pl.when(seg == segs - 2)
        def _():
            announce()

    for load in loads[:3]:
        load.wait()

    scale = HEAD_DIM ** (-0.5)
    lane = lax.broadcasted_iota(jnp.int32, (rows, QUAD), 1)
    heads = [jnp.logical_and(lane >= h * HEAD_DIM, lane < (h + 1) * HEAD_DIM).astype(F32)
             for h in range(4)]
    ones = [h.astype(BF) for h in heads]
    eighths = [(h * scale).astype(BF) for h in heads]
    left = lax.broadcasted_iota(jnp.int32, (rows, QUAD // 2), 1) < HEAD_DIM

    def masks(j):
        labels = jnp.broadcast_to(regs[j][...], (16, rows))
        onehot = (lax.broadcasted_iota(jnp.int32, (16, rows), 0) == labels).astype(F32)
        wide = jnp.concatenate([onehot] * 4, axis=1).astype(BF)
        same4[j] = mm(onehot.astype(BF), wide, 0, 0)

    def at(t, j):
        return (t * half + j) * rows

    def stack(x, by):
        return jnp.concatenate([x * h for h in by], axis=0)

    def fold(x):
        return jnp.concatenate(
            [jnp.where(left, x[2 * i * rows:(2 * i + 1) * rows, i * QUAD // 2:(i + 1) * QUAD // 2],
                       x[(2 * i + 1) * rows:(2 * i + 2) * rows, i * QUAD // 2:(i + 1) * QUAD // 2])
             for i in range(2)], axis=1)

    def part(ref, r, p, which):
        return ref[r:r + rows, which * width + p * QUAD:which * width + (p + 1) * QUAD]

    def softmax(ref, r, p, j):
        scores = mm(part(ref, r, p, 1), stack(part(ref, r, p, 0), eighths), 1, 1)
        scores = jnp.where(same4[j] > 0.5, scores, F32(-1000000000.0))
        e = jnp.exp(scores - jnp.max(scores, axis=0, keepdims=True))
        return e * (1.0 / jnp.sum(e, axis=0, keepdims=True))

    masks(0)
    for t in range(2):
        normal, inverse = stats(stash[0, t])
        norm32[t] = normal
        scales[t] = jnp.broadcast_to(inverse, (rows, 128))
        nrm[at(t, 0):at(t, 0) + rows] = normal.astype(BF)

    chain(seg == segs - 3)
    from_x(0)
    chain(seg < segs - 3)

    @pl.when(jnp.logical_and(encoder, seg < segs // 2 - 1))
    def _():
        skip_copy(0).start()

    for k in pieces[1:]:
        from_x(k)
    send_windows()
    for load in loads[3:]:
        load.wait()
    middle = len(pieces) // 2
    for k in pieces[:middle]:
        from_y(k)
    wo_from_x(0)
    for k in pieces[middle:-1]:
        from_y(k)
    wo_from_x(1)
    for k in pieces[-1:]:
        from_y(k)

    @pl.when(encoder)
    def _():
        skip_copy(1).start()

    from_mate(0, wqf)
    from_core()

    def w_qkv():
        return wqf[...].reshape(width, 3 * width)

    def w_out():
        return wof[...].reshape(width, width)

    def project(t, j):
        r = at(t, j)
        proj[r:r + rows] = mm(nrm[r:r + rows], w_qkv()).astype(BF)

    project(0, 0)

    def quad_backward(t, j, p, weights_f32, dctx):
        r = at(t, j)
        d4 = stack(dctx[:, p * QUAD:(p + 1) * QUAD], ones)
        d_attn = mm(part(proj, r, p, 2), d4, 1, 1)
        d_scores = (weights_f32 * (
            d_attn - jnp.sum(d_attn * weights_f32, axis=0, keepdims=True))).astype(BF)
        dq = fold(mm(d_scores, part(proj, r, p, 1), 0, 0)) * scale
        dk = mm(d_scores, stack(part(proj, r, p, 0), eighths))
        dv = mm(weights_f32.astype(BF), d4)
        for i, x in enumerate((dq, dk, dv)):
            dproj[r:r + rows, i * width + p * QUAD:i * width + (p + 1) * QUAD] = x.astype(BF)

    def context_of(ref, r, p, weights_f32):
        return fold(mm(weights_f32.astype(BF), part(ref, r, p, 2), 0, 0)).astype(BF)

    def input_cotangent(t):
        r = at(t, 0)
        d_norm = mm(dproj[r:r + rows], w_qkv(), 1, 1).astype(BF).astype(F32)
        normal, inverse = norm32[t], scales[t][:, 0:1]
        mean = jnp.mean(d_norm, axis=-1, keepdims=True)
        along = jnp.mean(d_norm * normal, axis=-1, keepdims=True)
        return (gall[t, 0].astype(F32) + inverse * (d_norm - mean - normal * along)).astype(BF)

    def forward(u):
        nrmf[...] = stats(u)[0].astype(BF)
        projf[...] = mm(nrmf[...], w_qkv()).astype(BF)
        outs = [context_of(projf, 0, p, softmax(projf, 0, p, 0)) for p in range(QUADS)]
        return (u.astype(F32) + mm(jnp.concatenate(outs, axis=1), w_out())).astype(BF)

    def d_ctx(t, j):
        return mm(gall[t, j], w_out(), 1, 1).astype(BF)

    quad = chip * 2 * depth // QUAD

    def attend(t, j):
        for p in range(QUADS):
            prob[t, j, p] = softmax(proj, at(t, j), p, j)

    def keep_context(t, j):
        r = at(t, j)
        values = proj[r:r + rows, pl.ds(pl.multiple_of(2 * width + quad * QUAD, QUAD), QUAD)]
        weights = prob[t, j, quad].astype(BF)
        ctx[r:r + rows] = fold(mm(weights, values, 0, 0)).astype(BF)

    def backward(t, j, dctx):
        for p in range(QUADS):
            quad_backward(t, j, p, prob[t, j, p], dctx)

    attend(0, 0)
    from_mate(1, wof)
    wo_from_core()
    dctx = d_ctx(0, 0)
    backward(0, 0, dctx)
    dsend[...] = input_cotangent(0)

    def d_copy(off):
        return remote(dsend, gall.at[1, off], dss.at[off], dsr.at[off],
                      segment=seg - 1, dp=peer(off) * 2 + core)

    @pl.when(seg > 0)
    def _():
        for off in range(half):
            d_copy(off).start()

    @pl.when(decoder)
    def _():
        skip_copy(0).wait_recv()
        joined[...] = (hid[...].astype(F32) + skin[0].astype(F32)).astype(BF)

    @pl.when(encoder)
    def _():
        joined[...] = hid[...]

    ysend[...] = forward(joined[...])

    def y_copy():
        return remote(ysend, yin, ysem.at[0], ysem.at[1], segment=seg + 1)

    @pl.when(seg < segs - 1)
    def _():
        y_copy().start()

    project(1, 0)
    attend(1, 0)

    def peer_window(t, j, copies):
        for copy in copies:
            copy.wait_recv()
        if t == 0:
            masks(j)
        r = at(t, j)
        nrm[r:r + rows] = stats(stash[j, t])[0].astype(BF)
        project(t, j)

    for j in range(1, half):
        peer_window(0, j, window_copies(j)[:3])
        attend(0, j)
        backward(0, j, d_ctx(0, j))
    for j in range(1, half):
        peer_window(1, j, window_copies(j)[3:])
        attend(1, j)
    for j in range(half):
        for t in range(2):
            keep_context(t, j)

    def columns_of(ref, first):
        if ref.shape[1] == 2 * depth:
            return ref[...]
        return ref[:, pl.ds(pl.multiple_of(first, 2 * depth), 2 * depth)]

    ready_rows = (half + 1) * rows
    for src, dest, first in ((nrm, nt, chip * 2 * depth), (ctx, ct, chip * 2 * depth - quad * QUAD)):
        block = columns_of(src, first)
        dest[0][...] = block[:ready_rows].T
        dest[1][...] = block[ready_rows:].T

    def cotangent_arrives(j):
        @pl.when(seg < segs - 1)
        def _():
            d_copy(j).wait_recv()

        @pl.when(last)
        def _():
            if j == 0:
                own_loss.wait()
            else:
                loss_copy(j).wait_recv()

    terms = [(o1s, o1r, okeep, 0)] + [
        (q1s.at[p], q1r.at[p], qkeep.at[p], 1 + p) for p in range(QUADS)]

    def hop(term):
        s1, r1, _, i = term
        return remote(s1, r1, p1s.at[i], p1r.at[i], dp=mate)

    def begin_term(term, left, right):
        keep = term[2]
        keep[...] = mm(left[0][...], right).reshape(keep.shape)

    def open_term(term, left, right):
        s1, _, keep, _ = term
        keep[...] = keep[...] + mm(left[1][...], right).reshape(keep.shape)
        s1[...] = keep[other].astype(BF)
        hop(term).start()

    for copy in sent:
        copy.wait_send()
    cotangent_arrives(0)
    dctx = d_ctx(1, 0)
    for p in range(QUADS):
        quad_backward(1, 0, p, prob[1, 0, p], dctx)
    grads[0] = input_cotangent(1)

    def projection_rows(p, first, last):
        return jnp.concatenate(
            [dproj[first:last, i * width + p * QUAD:i * width + (p + 1) * QUAD]
             for i in range(3)], axis=1)

    begin_term(terms[0], ct, jnp.concatenate(
        [gall[0].reshape(half * rows, width), gall[1, 0]], axis=0))
    for p in range(QUADS):
        begin_term(terms[1 + p], nt, projection_rows(p, 0, ready_rows))
    @pl.when(last)
    def _():
        for off in range(1, half):
            loss_copy(off).wait_send()

    @pl.when(encoder)
    def _():
        for t in range(2):
            skip_copy(t).wait_send()

    @pl.when(seg > 0)
    def _():
        for off in range(half):
            d_copy(off).wait_send()

    @pl.when(seg < segs - 1)
    def _():
        y_copy().wait_send()

    for j in range(1, half):
        cotangent_arrives(j)
    open_term(terms[0], ct, gall[1, 1:].reshape((half - 1) * rows, width))
    dctxs = [d_ctx(1, j) for j in range(1, half)]
    for p in range(QUADS):
        for j in range(1, half):
            quad_backward(1, j, p, prob[1, j, p], dctxs[j - 1])
        open_term(terms[1 + p], nt, projection_rows(p, ready_rows, 2 * half * rows))

    @pl.when(seg == 0)
    def _():
        joined[...] = ent[...]

    @pl.when(seg > 0)
    def _():
        y_copy().wait_recv()

    @pl.when(jnp.logical_and(seg > 0, encoder))
    def _():
        joined[...] = yin[...]

    @pl.when(decoder)
    def _():
        skip_copy(1).wait_recv()
        joined[...] = (yin[...].astype(F32) + skin[1].astype(F32)).astype(BF)

    acts[0] = forward(joined[...])

    def close_term(term):
        hop(term).wait_recv()
        return term[2][core] + term[1][...].astype(F32)

    go[0] = close_term(terms[0])
    for p in range(QUADS):
        total = close_term(terms[1 + p])
        for i in range(3):
            gq[0, :, i * width + p * QUAD:i * width + (p + 1) * QUAD] = (
                total[:, i * QUAD:(i + 1) * QUAD])

    for term in terms:
        hop(term).wait_send()


def solution(mesh):
    n, segs = mesh.shape["dp"], mesh.shape["segment"]
    half = n // 2
    in_specs = (
        P("segment", ("groups", "dp"), None),
        P("segment", None, ("groups", "dp"), None),
        P("segment", None, ("groups", "dp"), None),
        P("segment", ("groups", "dp"), None),
        P(None, ("groups", "dp"), None),
        P(None, ("groups", "dp"), None),
        P("segment", "dp", None),
        P("segment", "dp", None),
        P("segment", ("groups", "dp")),
    )
    out_specs = (
        P("segment", ("groups", "dp"), None),
        P("segment", ("groups", "dp"), None),
        P(("groups", "segment"), "dp", None),
        P(("groups", "segment"), "dp", None),
    )

    def step(hidden, stash, skip_store, cotan, entry, loss_grad, wqkv, wout, region):
        rows, width = hidden.shape[1:]
        depth = wqkv.shape[1]
        pieces = depth // 32
        vmem, dma = pltpu.VMEM, pltpu.SemaphoreType.DMA
        block = vmem((rows, width), BF)
        windows = 2 * half * rows

        outs = pl.pallas_call(
            functools.partial(kernel, n, segs),
            out_shape=(
                vmem(hidden.shape, BF), vmem(hidden.shape, BF),
                vmem(wqkv.shape, F32), vmem(wout.shape, F32),
            ),
            in_specs=[pl.BlockSpec(memory_space=pltpu.HBM)] * 9,
            out_specs=[pl.BlockSpec(memory_space=pltpu.VMEM)] * 4,
            scratch_shapes=[
                block, vmem((half, 2, rows, width), BF), block, vmem((2, half, rows, width), BF),
                [vmem(region.shape, region.dtype) for _ in range(half)], dma((8,)),
                vmem((n, depth, 3 * width), BF), vmem((n, depth, width), BF),
                vmem((2, rows, width), BF), block, block, block, block,
                vmem((windows, width), BF), block,
                vmem((windows, 3 * width), BF), vmem((rows, 3 * width), BF),
                *[[vmem((2 * depth, (half + 1) * rows), BF), vmem((2 * depth, (half - 1) * rows), BF)]] * 2,
                vmem((windows, 3 * width), BF), vmem((windows, QUAD), BF),
                vmem((2, half, QUADS, rows, 4 * rows), F32), vmem((half, rows, 4 * rows), F32),
                vmem((2, rows, width), F32), vmem((2, rows, 128), F32),
                *[vmem((QUADS, depth, 3 * QUAD), BF)] * 2, vmem((QUADS, 2, depth, 3 * QUAD), F32),
                *[vmem((depth, width), BF)] * 2, vmem((2, depth, width), F32),
                *[dma((half, pieces))] * 8, *[dma((half, 2))] * 4, dma((2,)), dma((2,)),
                dma((half, 5)), dma((half, 5)), dma((2,)), dma((2,)),
                dma((half,)), dma((half,)), dma((2,)),
                dma((QUADS + 1,)), dma((QUADS + 1,)), pltpu.SemaphoreType.REGULAR,
            ],
            compiler_params=pltpu.CompilerParams(
                collective_id=0, has_side_effects=True, vmem_limit_bytes=40 << 20),
        )(*[pltpu.with_memory_space_constraint(x, pltpu.HBM) for x in (
            hidden, stash, skip_store, cotan, entry, loss_grad, wqkv, wout, region)])
        return pl.pallas_call(
            flush,
            out_shape=tuple(jax.ShapeDtypeStruct(x.shape, x.dtype) for x in outs),
            in_specs=[pl.BlockSpec(memory_space=pltpu.VMEM)] * 4,
            out_specs=[pl.BlockSpec(memory_space=pltpu.HBM)] * 4,
            scratch_shapes=[dma((16,))],
            compiler_params=pltpu.CompilerParams(vmem_limit_bytes=16 << 20),
        )(*outs)

    return jax.shard_map(
        step, mesh=mesh, in_specs=in_specs, out_specs=out_specs, check_vma=False
    )
```
